128 devices in a mesh: seq: 32 (over z, y, core), tp: 4 (over x).
Axes of the slice: x: 4, y: 4, z: 4, core: 2. Of those that a mesh axis runs over, the one named last changes fastest.
Arguments:
- tokens: bfloat16 [65536, 2048], P('seq'), may hold values from -36 to 36
- gain: bfloat16 [2048], replicated, may hold values from 0.099609375 to 1.8984375
- w_in: bfloat16 [2048, 16, 160], P(None, 'tp'), may hold values from -0.125 to 0.125
- conv_taps: bfloat16 [3, 16, 160], P(None, 'tp'), may hold values from -2.5 to 2.5
- w_out: bfloat16 [2048, 2048], P(None, 'tp'), may hold values from -0.125 to 0.125
Outputs:
- result: bfloat16 [65536, 2048], P('seq', 'tp')
The draws below stay inside these ranges and needn't reach their ends.
All inputs are finite; a program needn't handle non-finite values.
Results may differ from the reference program's by a relative error of at most 0.014.
Values may be sent and summed in bfloat16 or wider, within the bound.
A program may use at most 128 MiB of HBM per device.

```python
import math
import jax
import jax.numpy as jnp
from jax import lax

D = 2048
H = 16
DK = 16
DV = 128
T_DEV = 2048
TOKENS = 65536
N_SEQ = 32


def draw_tokens(key, part):
    leading_key, second_key, third_key = jax.random.split(key, 3)
    row_scale = jnp.exp(jax.random.uniform(leading_key, (TOKENS, 1), minval=math.log(0.3), maxval=math.log(3.0)))
    column_scale = jnp.exp(jax.random.uniform(second_key, (1, D), minval=math.log(0.3), maxval=math.log(3.0)))
    starting_values = jnp.clip(jax.random.normal(third_key, (TOKENS, D)), -4.0, 4.0)
    return (starting_values * row_scale * column_scale).astype(jnp.bfloat16)


def block_levels(stream_key, dims, shards, least, top_value):
    level, own = 1.0, jax.random.fold_in(stream_key, 6)
    for position, blocks in shards:
        draws = jnp.exp(jax.random.uniform(jax.random.fold_in(own, position), (blocks,), jnp.float32, least / len(shards), top_value / len(shards)))
        level = level * jnp.repeat(draws, dims[position] // blocks).reshape([-1 if axis == position else 1 for axis in range(len(dims))])
    return level


def centred(key, shape, scale, bound, shards=(), dtype=jnp.bfloat16):
    level = block_levels(key, shape, shards, -0.22, 0.18) if shards else 1.0
    result = jax.random.normal(key, shape, jnp.float32) * scale * level
    return jnp.minimum(jnp.maximum(result, -bound), bound).astype(dtype)


def setup_inputs(seed: int = 0) -> dict:
    splits = jax.random.split(jax.random.key(seed), 6)
    tokens = draw_tokens(jax.random.fold_in(splits[5], 71), 0)
    gain = jnp.clip(1.0 + 0.18 * jax.random.normal(splits[1], (D,), jnp.float32), 0.099609375, 1.8984375).astype(jnp.bfloat16)
    w_in = centred(splits[2], (D, H, 2 * DK + DV), D ** -0.5, 0.125, ((1, 4),))
    conv_taps = centred(splits[3], (3, H, 2 * DK + DV), 0.6, 2.5, ((1, 4),))
    w_out = centred(splits[4], (H * DV, D), (H * DV) ** -0.5, 0.125, ((1, 4),))
    return {"tokens": tokens, "gain": gain, "w_in": w_in, "conv_taps": conv_taps, "w_out": w_out}


epsilon = 1e-06

def taylor_terms(mixed):
    queries = mixed[..., :DK]
    key_rows = mixed[..., DK:2 * DK]
    value_rows = mixed[..., 2 * DK:]
    factor = 1.0 / math.sqrt(DK)
    query_float = queries.astype(jnp.float32)
    key_float = key_rows.astype(jnp.float32)
    query_lin = (query_float * factor).astype(jnp.bfloat16)
    outer_query = query_float[..., :, None] * query_float[..., None, :] * (0.5 * factor * factor)
    query_sq = outer_query.reshape(outer_query.shape[:-2] + (DK * DK,)).astype(jnp.bfloat16)
    outer_key = key_float[..., :, None] * key_float[..., None, :]
    key_sq = outer_key.reshape(outer_key.shape[:-2] + (DK * DK,)).astype(jnp.bfloat16)
    return (queries, key_rows, value_rows, query_lin, query_sq, key_sq)

def reference(tokens, gain, w_in, conv_taps, w_out):
    token_float = tokens.astype(jnp.float32)
    mean_square = lax.optimization_barrier(jnp.mean(token_float * token_float, axis=-1, keepdims=True))
    normed = (token_float * lax.rsqrt(mean_square + epsilon) * gain.astype(jnp.float32)).astype(jnp.bfloat16)
    causal = jnp.arange(T_DEV)[:, None] >= jnp.arange(T_DEV)[None, :]
    factor = 1.0 / math.sqrt(DK)
    columns = 2 * DK + DV

    def one_head(operands):
        weight_head, taps = operands
        projected = jnp.dot(normed, weight_head, preferred_element_type=jnp.float32).astype(jnp.bfloat16)
        padded = jnp.concatenate([jnp.zeros((2, columns), jnp.bfloat16), projected], 0)
        tap_float = taps.astype(jnp.float32)
        mixed = (padded[:-2] * tap_float[0] + padded[1:-1] * tap_float[1] + padded[2:] * tap_float[2]).astype(jnp.bfloat16)
        terms = taylor_terms(mixed)
        blocked = tuple((member.reshape(N_SEQ, T_DEV, member.shape[-1]) for member in terms))

        def block_step(running, block_terms):
            query_blk, key_block, value_blk, lin_blk, square_blk, key_square_block = block_terms
            prefix_low = tuple((member.astype(jnp.bfloat16) for member in running))
            scores = jnp.dot(query_blk, key_block.T, preferred_element_type=jnp.float32) * factor
            weights = jnp.where(causal, 1.0 + scores + 0.5 * scores * scores, 0.0).astype(jnp.bfloat16)
            numerator = jnp.dot(weights, value_blk, preferred_element_type=jnp.float32)
            numerator = numerator + prefix_low[0].astype(jnp.float32)[None, :]
            numerator = numerator + jnp.dot(lin_blk, prefix_low[1], preferred_element_type=jnp.float32)
            numerator = numerator + jnp.dot(square_blk, prefix_low[2], preferred_element_type=jnp.float32)
            spread = lax.optimization_barrier(jnp.mean(numerator * numerator, axis=-1, keepdims=True))
            head_out = (numerator * lax.rsqrt(spread + epsilon)).astype(jnp.bfloat16)
            updated = (running[0] + lax.optimization_barrier(jnp.sum(value_blk.astype(jnp.float32), 0)), running[1] + jnp.dot(key_block.T, value_blk, preferred_element_type=jnp.float32), running[2] + jnp.dot(key_square_block.T, value_blk, preferred_element_type=jnp.float32))
            return (updated, head_out)
        initial = (jnp.zeros((DV,), jnp.float32), jnp.zeros((DK, DV), jnp.float32), jnp.zeros((DK * DK, DV), jnp.float32))
        final_state, outputs = lax.scan(block_step, initial, blocked)
        return outputs.reshape(TOKENS, DV)
    per_head = lax.map(one_head, (jnp.moveaxis(w_in, 1, 0), jnp.moveaxis(conv_taps, 1, 0)))
    joined = jnp.moveaxis(per_head, 0, 1).reshape(TOKENS, H * DV)
    return jnp.dot(joined, w_out, preferred_element_type=jnp.float32).astype(jnp.bfloat16)
```

```python
import functools
import math

import jax
import jax.numpy as jnp
import numpy as np
from jax import lax
from jax.experimental import pallas as pl
from jax.experimental.pallas import tpu as pltpu
from jax.sharding import PartitionSpec as P

DK = 16
DV = 128
HL = 4
T = 2048
D = 2048
C = 256
NC = T // C
F = 160
FP = 256
VW = HL * DV
QW = HL * 2 * DK
SEQ = 32
TP = 4
CHIPS = SEQ // 2
ROWS = HL * F // CHIPS
EPS = 1e-06
MESH = pl.DeviceIdType.MESH
F32 = jnp.float32
BF16 = jnp.bfloat16


def feature_maps():
    eq = np.zeros((2, FP, HL * FP), np.float32)
    ek = np.zeros((2, HL * F, FP), np.float32)
    one = QW
    for h in range(HL):
        q0, k0 = 2 * DK * h, 2 * DK * h + DK
        f = 0
        for i in range(DK):
            for j in range(i, DK):
                eq[0, q0 + i, h * FP + f] = (1.0 if i == j else 2.0) / 32.0
                eq[1, q0 + j, h * FP + f] = 1.0
                ek[0, h * F + f, k0 + i] = 1.0
                ek[1, h * F + f, k0 + j] = 1.0
                f += 1
        for i in range(DK):
            eq[0, q0 + i, h * FP + f] = 0.25
            eq[1, one, h * FP + f] = 1.0
            ek[0, h * F + f, k0 + i] = 1.0
            ek[1, h * F + f, one] = 1.0
            f += 1
        eq[0, one, h * FP + f] = 1.0
        eq[1, one, h * FP + f] = 1.0
        ek[0, h * F + f, one] = 1.0
        ek[1, h * F + f, one] = 1.0
    return eq.astype(jnp.bfloat16), ek.astype(jnp.bfloat16)


def kernel(
    x_hbm, gain_ref, wt_hbm, taps_ref, wo_hbm, eq_hbm, ek_hbm,
    out_ref,
    xv, wv, eqv, ekv, taps, pf, vb, qk, kt, sc, nl, pq, sb, r1, p2, r2, pp, wf, ho, g, ob,
    in_sem, x_sem, wo_sem, halo_s, halo_r, s1_s, s1_r, s2_s, s2_r, s3_s, s3_r,
    wx_s, wx_r, wa_s, wa_r, wb_s, wb_r, wc_s, wc_r, a_s, a_r, b_s, b_r, own_s,
):
    s = lax.axis_index("seq")
    t = lax.axis_index("tp")
    chip = s // 2
    core = s % 2
    zc = s // 8
    yc = (s // 2) % 4
    sib = s + 1 - 2 * core

    def remote(src, dst, ss, rs, dev):
        return pltpu.make_async_remote_copy(
            src_ref=src, dst_ref=dst, send_sem=ss, recv_sem=rs, device_id=dev, device_id_type=MESH
        )

    def xpeer(d):
        return (s, lax.rem(t + d, TP))

    def ypeer(d):
        return (zc * 8 + lax.rem(yc + d, 4) * 2 + core, t)

    def zpeer(d):
        return (lax.rem(zc + d, 4) * 8 + yc * 2 + core, t)

    wcopy = pltpu.make_async_copy(wt_hbm, wv, in_sem.at[0])
    wcopy.start()
    order = [NC - 1] + list(range(NC - 1))
    xcopies = {}
    for c in order:
        xcopies[c] = pltpu.make_async_copy(x_hbm.at[pl.ds(c * C, C)], xv.at[pl.ds(c * C, C)], x_sem.at[c])
        xcopies[c].start()
    ekcopy = pltpu.make_async_copy(ek_hbm, ekv, in_sem.at[1])
    ekcopy.start()
    eqcopy = pltpu.make_async_copy(eq_hbm, eqv, in_sem.at[2])
    eqcopy.start()
    wocopies = [
        pltpu.make_async_copy(
            wo_hbm.at[zz, yy, cc], wf.at[0, zz, yy, cc], wo_sem
        )
        for zz in range(0) for yy in range(0) for cc in range(0)
    ]
    wocopy = pltpu.make_async_copy(wo_hbm, wf.at[0], wo_sem)
    wocopy.start()

    barrier = pltpu.get_barrier_semaphore()

    def greet(j, carry):
        pl.semaphore_signal(barrier, inc=1, device_id=(lax.rem(s + j, SEQ), t), device_id_type=MESH)
        return carry

    lax.fori_loop(1, SEQ, greet, 0)
    for d in range(1, TP):
        pl.semaphore_signal(barrier, inc=1, device_id=xpeer(d), device_id_type=MESH)

    row = lax.broadcasted_iota(jnp.int32, (160, 128), 0)
    col = lax.broadcasted_iota(jnp.int32, (160, 128), 1)
    pick_v = (row == col + 2 * DK).astype(F32).astype(BF16)
    for k in range(3):
        tk = taps_ref[k]
        tv = jnp.dot(tk, pick_v, preferred_element_type=F32)
        tq = jnp.zeros((1, QW), F32)
        for h in range(HL):
            taps[k : k + 1, h * DV : (h + 1) * DV] = tv[h : h + 1, :]
            pick_q = ((row + 2 * DK * h == col) & (row < 2 * DK)).astype(F32).astype(BF16)
            tq = tq + jnp.dot(tk, pick_q, preferred_element_type=F32)[h : h + 1, :]
        taps[k : k + 1, VW:] = tq

    wcopy.wait()
    gain = gain_ref[...].astype(F32)
    wg = wv
    for r in range(0, HL * 160, 32):
        wg[r : r + 32, :] = (wv[r : r + 32, :].astype(F32) * gain).astype(BF16)

    def project(c):
        xt = xv[c * C : (c + 1) * C, :]
        xf = xt.astype(F32)
        scale = lax.rsqrt(jnp.mean(xf * xf, axis=-1, keepdims=True) + EPS)
        pr = lax.dot_general(xt, wg[...], (((1,), (1,)), ((), ())), preferred_element_type=F32)
        pr = (pr * scale).astype(BF16).astype(F32)
        base = 8 + c * C
        for h in range(HL):
            pf[base : base + C, h * DV : (h + 1) * DV] = pr[:, h * 160 + 32 : h * 160 + 160]
            pf[base : base + C, VW + 32 * h : VW + 32 * h + 32] = pr[:, h * 160 : h * 160 + 32]

    xcopies[NC - 1].wait()
    project(NC - 1)

    pl.semaphore_wait(barrier, SEQ - 1 + TP - 1)
    halo = remote(
        pf.at[pl.ds(T, 8)], pf.at[pl.ds(0, 8)], halo_s, halo_r, (lax.rem(s + 1, SEQ), t)
    )
    halo.start()
    wx = []
    for d in range(1, TP):
        cp = remote(
            wo_hbm.at[zc, yc, core], wf.at[TP - d, zc, yc, core], wx_s.at[d - 1], wx_r.at[d - 1], xpeer(d)
        )
        cp.start()
        wx.append(cp)

    def states(c):
        ext = pf[c * C : c * C + C + 8, :]
        mixed = (
            ext[6 : 6 + C] * taps[0:1, :] + ext[7 : 7 + C] * taps[1:2, :] + ext[8 : 8 + C] * taps[2:3, :]
        )
        vb[c * C : (c + 1) * C, :] = mixed[:, :VW].astype(BF16)
        qkb = mixed[:, VW:].astype(BF16)
        qk[c * C : (c + 1) * C, :] = qkb
        qt = jnp.transpose(qkb.astype(F32)).astype(BF16)
        kt[c] = qt
        qe = jnp.concatenate([qt, jnp.ones((FP - QW, C), BF16)], axis=0)
        fk = (
            jnp.dot(ekv[0], qe, preferred_element_type=F32) * jnp.dot(ekv[1], qe, preferred_element_type=F32)
        ).astype(BF16)
        for h in range(HL):
            sc[c, h * F : (h + 1) * F, :] = jnp.dot(
                fk[h * F : (h + 1) * F, :], vb[c * C : (c + 1) * C, h * DV : (h + 1) * DV],
                preferred_element_type=F32,
            )

    ekcopy.wait()
    for c in range(NC - 1):
        xcopies[c].wait()
        project(c)
        if c >= 1:
            states(c)
    states(NC - 1)

    for cp in wx:
        cp.wait()
    wa = []
    for d in range(1, 4):
        src = wf.at[1:4, zc, yc, core, :, 0:256]
        cp = remote(src, src, wa_s.at[d - 1], wa_r.at[d - 1], ypeer(d))
        cp.start()
        wa.append(cp)
        src = wf.at[1:4, zc, yc, core, :, 256:512]
        cp = remote(src, src, wa_s.at[d + 2], wa_r.at[d + 2], zpeer(d))
        cp.start()
        wa.append(cp)

    halo.wait()
    pf[0:8, :] = jnp.where(s == 0, 0.0, pf[0:8, :])
    states(0)

    run = jnp.zeros((HL * F, DV), F32)
    for c in range(NC):
        part = sc[c]
        sc[c] = run
        run = run + part
    for k in range(CHIPS):
        sb[k] = run[k * ROWS : (k + 1) * ROWS, :].astype(BF16)

    def spread(i, carry):
        k = lax.rem(chip + i, CHIPS)
        remote(sb.at[k], r1.at[s], s1_s, s1_r, (2 * k, t)).start()
        return carry

    lax.fori_loop(1, CHIPS, spread, 0)

    @pl.when(core == 1)
    def _():
        cp = remote(sb.at[chip], r1.at[s], s3_s, s1_r, (s - 1, t))
        cp.start()
        cp.wait_send()

    @pl.when(core == 0)
    def _():
        r1[s] = sb[chip]

    eqcopy.wait()
    pos = lax.broadcasted_iota(jnp.int32, (C, C), 0) >= lax.broadcasted_iota(jnp.int32, (C, C), 1)

    def local(c):
        q = qk[c * C : (c + 1) * C, :]
        qe = jnp.concatenate([q, jnp.ones((C, FP - QW), BF16)], axis=1)
        ktc = (kt[c].astype(F32) * 0.25).astype(BF16)
        for h in range(HL):
            fq = (
                jnp.dot(qe, eqv[0, :, h * FP : (h + 1) * FP], preferred_element_type=F32)
                * jnp.dot(qe, eqv[1, :, h * FP : (h + 1) * FP], preferred_element_type=F32)
            ).astype(BF16)
            pq[c * C : (c + 1) * C, h * FP : (h + 1) * FP] = fq
            parts = []
            if h > 0:
                parts.append(jnp.zeros((32 * h, C), BF16))
            parts.append(ktc[32 * h + 16 : 32 * h + 32, :])
            parts.append(jnp.zeros((QW - 32 * h - 16, C), BF16))
            keys = jnp.concatenate(parts, axis=0)
            up = jnp.dot(q, keys, preferred_element_type=F32) + 1.0
            w = jnp.where(pos, up * up * 0.5 + 0.5, 0.0).astype(BF16)
            num = jnp.dot(w, vb[c * C : (c + 1) * C, h * DV : (h + 1) * DV], preferred_element_type=F32)
            if c > 0:
                before = jnp.concatenate(
                    [sc[c, h * F : (h + 1) * F, :].astype(BF16), jnp.zeros((FP - F, DV), BF16)], axis=0
                )
                num = num + jnp.dot(fq, before, preferred_element_type=F32)
            nl[c * C : (c + 1) * C, h * DV : (h + 1) * DV] = num

    for c in range(NC // 2):
        local(c)

    @pl.when(core == 0)
    def _():
        pltpu.make_async_copy(r1.at[0 : SEQ - 1], r1.at[0 : SEQ - 1], s1_r).wait()
        acc = jnp.zeros((ROWS, DV), F32)
        for k in range(SEQ):
            p2[k // 2, k % 2] = acc.astype(BF16)
            acc = acc + r1[k].astype(F32)
        r2[chip] = p2[chip]

        def back(i, carry):
            k = lax.rem(chip + i, CHIPS)
            remote(p2.at[k], r2.at[chip], s2_s, s2_r, (2 * k, t)).start()
            return carry

        lax.fori_loop(1, CHIPS, back, 0)

    pltpu.make_async_copy(sb.at[0 : CHIPS - 1], sb.at[0 : CHIPS - 1], s1_s).wait()
    for c in range(NC // 2, NC):
        local(c)

    for cp in wa:
        cp.wait()
    wb = []
    for d in range(1, 4):
        src = wf.at[1:4, zc, :, core, :, 0:256]
        cp = remote(src, src, wb_s.at[d - 1], wb_r.at[d - 1], zpeer(d))
        cp.start()
        wb.append(cp)
        src = wf.at[1:4, :, yc, core, :, 256:512]
        cp = remote(src, src, wb_s.at[d + 2], wb_r.at[d + 2], ypeer(d))
        cp.start()
        wb.append(cp)

    fwd = remote(r2, r2, s3_s, s3_r, (sib, t))

    @pl.when(core == 0)
    def _():
        pltpu.make_async_copy(p2.at[0 : CHIPS - 1], p2.at[0 : CHIPS - 1], s2_s).wait()
        pltpu.make_async_copy(r2.at[0 : CHIPS - 1], r2.at[0 : CHIPS - 1], s2_r).wait()
        fwd.start()

    @pl.when(core == 1)
    def _():
        fwd.wait_recv()

    pp[...] = jnp.zeros_like(pp)
    for k in range(CHIPS):
        h, o = k // 4, (k % 4) * ROWS
        pp[h, o : o + ROWS, :] = r2[k, core]

    def finish(i, dst):
        base = pl.multiple_of(i * C, C)
        for h in range(HL):
            num = nl[pl.ds(base, C), h * DV : (h + 1) * DV] + jnp.dot(
                pq[pl.ds(base, C), h * FP : (h + 1) * FP], pp[h], preferred_element_type=F32
            )
            spread_ = jnp.mean(num * num, axis=-1, keepdims=True)
            dst[:, h * DV : (h + 1) * DV] = (num * lax.rsqrt(spread_ + EPS)).astype(BF16)

    sent = {}
    for half in range(2):
        for n, d in enumerate((1, 3, 2)):
            owner = lax.rem(t + d, TP)
            finish(owner * 2 + half, ho.at[half, n])
            cp = remote(
                ho.at[half, n], g.at[t, half], a_s.at[half, n], a_r.at[half, d - 1], (s, owner)
            )
            cp.start()
            sent[half, n] = cp
        finish(t * 2 + half, g.at[t, half])

    @pl.when(core == 0)
    def _():
        fwd.wait_send()

    for cp in wb:
        cp.wait()
    src = wf.at[1:4, :, :, core]
    wc = remote(src, src, wc_s, wc_r, (sib, t))
    wc.start()
    wocopy.wait()
    wc.wait()

    results = []
    own = []
    for half in range(2):
        for d in range(1, TP):
            remote(
                ho.at[half, 0], g.at[lax.rem(t + TP - d, TP), half], a_s.at[half, 0], a_r.at[half, d - 1], xpeer(d)
            ).wait_recv()
        for n, d in enumerate((1, 3, 2, 0)):
            acc = jnp.zeros((C, 512), F32)
            for p in range(TP):
                acc = acc + jnp.dot(
                    g[p, half], wf[d, p].reshape(512, 512), preferred_element_type=F32
                )
            ob[half, n] = acc.astype(BF16)
            rows = out_ref.at[pl.ds(pl.multiple_of(t * 512 + half * C, C), C)]
            if d:
                cp = remote(ob.at[half, n], rows, b_s.at[half, n], b_r.at[half, d - 1], xpeer(d))
                cp.start()
                results.append(cp)
            else:
                cp = pltpu.make_async_copy(ob.at[half, n], rows, own_s.at[half])
                cp.start()
                own.append(cp)

    for cp in sent.values():
        cp.wait_send()
    for cp in results:
        cp.wait_send()
    for half in range(2):
        for d in range(1, TP):
            src_t = lax.rem(t + TP - d, TP)
            rows = out_ref.at[pl.ds(pl.multiple_of(src_t * 512 + half * C, C), C)]
            remote(ob.at[half, 0], rows, b_s.at[half, 0], b_r.at[half, d - 1], xpeer(d)).wait_recv()
    for cp in own:
        cp.wait()


def body(tokens, gain, w_in, conv_taps, w_out):
    wt = jnp.transpose(w_in, (1, 2, 0)).reshape(HL * 160, D)
    eq, ek = feature_maps()
    hbm = pl.BlockSpec(memory_space=pl.ANY)
    vmem = pl.BlockSpec(memory_space=pltpu.VMEM)
    dma = pltpu.SemaphoreType.DMA
    return pl.pallas_call(
        kernel,
        out_shape=jax.ShapeDtypeStruct((T, 512), BF16),
        in_specs=[hbm, vmem, hbm, vmem, hbm, hbm, hbm],
        out_specs=hbm,
        scratch_shapes=[
            pltpu.VMEM((T, D), BF16),
            pltpu.VMEM((HL * 160, D), BF16),
            pltpu.VMEM((2, FP, HL * FP), BF16),
            pltpu.VMEM((2, HL * F, FP), BF16),
            pltpu.VMEM((8, VW + QW), F32),
            pltpu.VMEM((8 + T, VW + QW), F32),
            pltpu.VMEM((T, VW), BF16),
            pltpu.VMEM((T, QW), BF16),
            pltpu.VMEM((NC, QW, C), BF16),
            pltpu.VMEM((NC, HL * F, DV), F32),
            pltpu.VMEM((T, VW), F32),
            pltpu.VMEM((T, HL * FP), BF16),
            pltpu.VMEM((CHIPS, ROWS, DV), BF16),
            pltpu.VMEM((SEQ, ROWS, DV), BF16),
            pltpu.VMEM((CHIPS, 2, ROWS, DV), BF16),
            pltpu.VMEM((CHIPS, 2, ROWS, DV), BF16),
            pltpu.VMEM((HL, FP, DV), BF16),
            pltpu.VMEM((4, 4, 4, 2, 64, 512), BF16),
            pltpu.VMEM((2, 3, C, VW), BF16),
            pltpu.VMEM((TP, 2, C, VW), BF16),
            pltpu.VMEM((2, 4, C, 512), BF16),
            dma((3,)), dma((NC,)), dma, dma, dma, dma, dma, dma, dma, dma, dma,
            dma((3,)), dma((3,)), dma((6,)), dma((6,)), dma((6,)), dma((6,)), dma, dma,
            dma((2, 3)), dma((2, 3)), dma((2, 4)), dma((2, 3)), dma((2,)),
        ],
        compiler_params=pltpu.CompilerParams(
            collective_id=0, has_side_effects=True, vmem_limit_bytes=60 * 1024 * 1024
        ),
    )(
        tokens, gain.reshape(1, D), wt, conv_taps, w_out.reshape(4, 4, 2, 64, 512),
        jnp.asarray(eq), jnp.asarray(ek),
    )


def solution(mesh):
    return jax.shard_map(
        body,
        mesh=mesh,
        in_specs=(P("seq", None), P(), P(None, "tp", None), P(None, "tp", None), P(None, "tp")),
        out_specs=P("seq", "tp"),
        check_vma=False,
    )
```

```python
import functools
import math

import jax
import jax.numpy as jnp
import numpy as np
from jax import lax
from jax.experimental import pallas as pl
from jax.experimental.pallas import tpu as pltpu
from jax.sharding import PartitionSpec as P

DK = 16
DV = 128
HL = 4
T = 2048
D = 2048
C = 256
NC = T // C
F = 160
FP = 256
VW = HL * DV
QW = HL * 2 * DK
SEQ = 32
TP = 4
CHIPS = SEQ // 2
ROWS = HL * F // CHIPS
EPS = 1e-06
MESH = pl.DeviceIdType.MESH
F32 = jnp.float32
BF16 = jnp.bfloat16


def feature_maps():
    eq = np.zeros((2, FP, HL * FP), np.float32)
    ek = np.zeros((2, HL * F, FP), np.float32)
    one = QW
    for h in range(HL):
        q0, k0 = 2 * DK * h, 2 * DK * h + DK
        f = 0
        for i in range(DK):
            for j in range(i, DK):
                eq[0, q0 + i, h * FP + f] = (1.0 if i == j else 2.0) / 32.0
                eq[1, q0 + j, h * FP + f] = 1.0
                ek[0, h * F + f, k0 + i] = 1.0
                ek[1, h * F + f, k0 + j] = 1.0
                f += 1
        for i in range(DK):
            eq[0, q0 + i, h * FP + f] = 0.25
            eq[1, one, h * FP + f] = 1.0
            ek[0, h * F + f, k0 + i] = 1.0
            ek[1, h * F + f, one] = 1.0
            f += 1
        eq[0, one, h * FP + f] = 1.0
        eq[1, one, h * FP + f] = 1.0
        ek[0, h * F + f, one] = 1.0
        ek[1, h * F + f, one] = 1.0
    return eq.astype(jnp.bfloat16), ek.astype(jnp.bfloat16)


def kernel(
    x_hbm, gain_ref, wt_hbm, taps_ref, wo_hbm, eq_hbm, ek_hbm,
    out_ref,
    xv, xt8, wv, wg, eqv, ekv, taps, pf, tl, mx, ga, sc, nl, fq, sb, r1, p2, r2, ps, pp, wf, gh, ob,
    in_sem, x_sem, wo_sem, halo_s, halo_r, s1_s, s1_r, s2_s, s2_r, s3_s, s3_r,
    wx_s, wx_r, wa_s, wa_r, wb_s, wb_r, wc_s, wc_r, a_s, a_r, q_s, q_r, b_s, b_r, own_s,
):
    s = lax.axis_index("seq")
    t = lax.axis_index("tp")
    chip = s // 2
    core = s % 2
    zc = s // 8
    yc = (s // 2) % 4
    sib = s + 1 - 2 * core

    def remote(src, dst, ss, rs, dev):
        return pltpu.make_async_remote_copy(
            src_ref=src, dst_ref=dst, send_sem=ss, recv_sem=rs, device_id=dev, device_id_type=MESH
        )

    def near(d):
        return lax.rem(t + d, TP)

    def xpeer(d):
        return (s, near(d))

    def ypeer(d):
        return (zc * 8 + lax.rem(yc + d, 4) * 2 + core, t)

    def zpeer(d):
        return (lax.rem(zc + d, 4) * 8 + yc * 2 + core, t)

    tiles = [(d, half) for half in (1, 0) for d in (1, 3, 2)] + [(0, 1), (0, 0)]

    wcopy = pltpu.make_async_copy(wt_hbm, wv, in_sem.at[0])
    wcopy.start()
    tcopies = []
    for c in range(NC):
        cp = pltpu.make_async_copy(x_hbm.at[pl.ds(c * C + C - 8, 8)], xt8.at[pl.ds(8 * c, 8)], in_sem.at[3 + c])
        cp.start()
        tcopies.append(cp)
    xcopies = []
    for i, (d, half) in enumerate(tiles):
        base = pl.multiple_of((near(d) * 2 + half) * C, C)
        cp = pltpu.make_async_copy(x_hbm.at[pl.ds(base, C)], xv.at[i], x_sem.at[i])
        cp.start()
        xcopies.append(cp)
    ekcopy = pltpu.make_async_copy(ek_hbm, ekv, in_sem.at[1])
    ekcopy.start()
    eqcopy = pltpu.make_async_copy(eq_hbm, eqv, in_sem.at[2])
    eqcopy.start()
    wocopy = pltpu.make_async_copy(wo_hbm, wf.at[0], wo_sem)
    wocopy.start()

    barrier = pltpu.get_barrier_semaphore()

    def greet(j, carry):
        pl.semaphore_signal(barrier, inc=1, device_id=(lax.rem(s + j, SEQ), t), device_id_type=MESH)
        return carry

    lax.fori_loop(1, SEQ, greet, 0)
    for d in range(1, TP):
        pl.semaphore_signal(barrier, inc=1, device_id=xpeer(d), device_id_type=MESH)

    pp[:, :, F:, :] = jnp.zeros((TP, HL, FP - F, DV), BF16)

    row = lax.broadcasted_iota(jnp.int32, (160, 128), 0)
    col = lax.broadcasted_iota(jnp.int32, (160, 128), 1)
    pick_v = (row == col + 2 * DK).astype(F32).astype(BF16)
    for k in range(3):
        tk = taps_ref[k]
        tv = jnp.dot(tk, pick_v, preferred_element_type=F32)
        tq = jnp.zeros((1, QW), F32)
        for h in range(HL):
            taps[k : k + 1, h * DV : (h + 1) * DV] = tv[h : h + 1, :]
            pick_q = ((row + 2 * DK * h == col) & (row < 2 * DK)).astype(F32).astype(BF16)
            tq = tq + jnp.dot(tk, pick_q, preferred_element_type=F32)[h : h + 1, :]
        taps[k : k + 1, VW:] = tq

    wcopy.wait()
    gain = gain_ref[...].astype(F32)
    for h in range(HL):
        for r in range(0, 160, 32):
            dst = VW + 32 * h if r == 0 else h * DV + r - 32
            src = h * 160 + r
            wg[dst : dst + 32, :] = (wv[src : src + 32, :].astype(F32) * gain).astype(BF16)

    def project(xt):
        xf = xt.astype(F32)
        scale = lax.rsqrt(jnp.mean(xf * xf, axis=-1, keepdims=True) + EPS)
        pr = lax.dot_general(xt, wg[...], (((1,), (1,)), ((), ())), preferred_element_type=F32)
        return (pr * scale).astype(BF16).astype(F32)

    for cp in tcopies:
        cp.wait()
    tl[8:, :] = project(xt8[...])

    pl.semaphore_wait(barrier, SEQ - 1 + TP - 1)
    halo = remote(tl.at[pl.ds(8 * NC, 8)], tl.at[pl.ds(0, 8)], halo_s, halo_r, (lax.rem(s + 1, SEQ), t))
    halo.start()
    wx = []
    for d in range(1, TP):
        cp = remote(
            wo_hbm.at[zc, yc, core], wf.at[TP - d, zc, yc, core], wx_s.at[d - 1], wx_r.at[d - 1], xpeer(d)
        )
        cp.start()
        wx.append(cp)

    def mix(i, c, dst):
        buf = pf.at[i % 2]
        buf[0:8, :] = tl[pl.ds(pl.multiple_of(c * 8, 8), 8), :]
        buf[8:, :] = project(xv[i])
        mixed = (
            buf[6 : 6 + C, :] * taps[0:1, :] + buf[7 : 7 + C, :] * taps[1:2, :] + buf[8 : 8 + C, :] * taps[2:3, :]
        )
        dst[...] = mixed.astype(BF16)

    def states(c, src):
        qe = jnp.concatenate(
            [jnp.transpose(src[:, VW:].astype(F32)).astype(BF16), jnp.ones((FP - QW, C), BF16)], axis=0
        )
        fk = (
            jnp.dot(ekv[0], qe, preferred_element_type=F32) * jnp.dot(ekv[1], qe, preferred_element_type=F32)
        ).astype(BF16)
        for h in range(HL):
            sc[c, h * F : (h + 1) * F, :] = jnp.dot(
                fk[h * F : (h + 1) * F, :], src[:, h * DV : (h + 1) * DV], preferred_element_type=F32
            )

    ekcopy.wait()
    sent = []
    wa = []
    for i, (d, half) in enumerate(tiles):
        c = near(d) * 2 + half
        if i == 3:
            halo.wait()
            tl[0:8, :] = jnp.where(s == 0, 0.0, tl[0:8, :])
        if i == 4:
            for cp in wx:
                cp.wait()
            for n in range(1, 4):
                src = wf.at[1:4, zc, yc, core, :, 0:256]
                cp = remote(src, src, wa_s.at[n - 1], wa_r.at[n - 1], ypeer(n))
                cp.start()
                wa.append(cp)
                src = wf.at[1:4, zc, yc, core, :, 256:512]
                cp = remote(src, src, wa_s.at[n + 2], wa_r.at[n + 2], zpeer(n))
                cp.start()
                wa.append(cp)
        xcopies[i].wait()
        tile = mx.at[i] if d else ga.at[t, half]
        mix(i, c, tile)
        if d:
            cp = remote(tile, ga.at[t, half], a_s.at[half, d - 1], a_r.at[half, d - 1], xpeer(d))
            cp.start()
            sent.append(cp)
        states(c, tile)

    run = jnp.zeros((HL * F, DV), F32)
    for c in range(NC):
        part = sc[c]
        if c % 2 == 0:
            sc[c] = run
        run = run + part
    for k in range(CHIPS):
        sb[k] = run[k * ROWS : (k + 1) * ROWS, :].astype(BF16)

    def spread(i, carry):
        k = lax.rem(chip + i, CHIPS)
        remote(sb.at[k], r1.at[s], s1_s, s1_r, (2 * k, t)).start()
        return carry

    lax.fori_loop(1, CHIPS, spread, 0)

    @pl.when(core == 1)
    def _():
        cp = remote(sb.at[chip], r1.at[s], s3_s, s1_r, (s - 1, t))
        cp.start()
        cp.wait_send()

    @pl.when(core == 0)
    def _():
        r1[s] = sb[chip]

    for cp in wa:
        cp.wait()
    wb = []
    for d in range(1, 4):
        src = wf.at[1:4, zc, :, core, :, 0:256]
        cp = remote(src, src, wb_s.at[d - 1], wb_r.at[d - 1], zpeer(d))
        cp.start()
        wb.append(cp)
        src = wf.at[1:4, :, yc, core, :, 256:512]
        cp = remote(src, src, wb_s.at[d + 2], wb_r.at[d + 2], ypeer(d))
        cp.start()
        wb.append(cp)

    eqcopy.wait()
    pos = lax.broadcasted_iota(jnp.int32, (C, C), 0) >= lax.broadcasted_iota(jnp.int32, (C, C), 1)

    def arrived(d, half):
        n = TP - d - 1
        remote(mx.at[0], ga.at[near(d), half], a_s.at[half, n], a_r.at[half, n], xpeer(d)).wait_recv()

    def scores(q, kt, h):
        parts = []
        if h > 0:
            parts.append(jnp.zeros((32 * h, C), BF16))
        parts.append(kt[32 * h + 16 : 32 * h + 32, :])
        parts.append(jnp.zeros((QW - 32 * h - 16, C), BF16))
        up = jnp.dot(q, jnp.concatenate(parts, axis=0), preferred_element_type=F32) + 1.0
        return up * up * 0.5 + 0.5

    def keys(src):
        return (jnp.transpose(src[:, VW:].astype(F32)) * 0.25).astype(BF16)

    def local(d, half):
        src = ga.at[near(d), half]
        q = src[:, VW:]
        qe = jnp.concatenate([q, jnp.ones((C, FP - QW), BF16)], axis=1)
        kt = keys(src)
        for h in range(HL):
            fq[half, d, :, h * FP : (h + 1) * FP] = (
                jnp.dot(qe, eqv[0, :, h * FP : (h + 1) * FP], preferred_element_type=F32)
                * jnp.dot(qe, eqv[1, :, h * FP : (h + 1) * FP], preferred_element_type=F32)
            ).astype(BF16)
            w = jnp.where(pos, scores(q, kt, h), 0.0).astype(BF16)
            nl[half, d, :, h * DV : (h + 1) * DV] = jnp.dot(
                w, src[:, h * DV : (h + 1) * DV], preferred_element_type=F32
            )

    def across(d):
        q = ga[near(d), 1, :, VW:]
        src = ga.at[near(d), 0]
        kt = keys(src)
        for h in range(HL):
            w = scores(q, kt, h).astype(BF16)
            nl[1, d, :, h * DV : (h + 1) * DV] += jnp.dot(
                w, src[:, h * DV : (h + 1) * DV], preferred_element_type=F32
            )

    local(0, 1)
    local(0, 0)
    across(0)

    @pl.when(core == 0)
    def _():
        pltpu.make_async_copy(r1.at[0 : SEQ - 1], r1.at[0 : SEQ - 1], s1_r).wait()
        acc = jnp.zeros((ROWS, DV), F32)
        for k in range(SEQ):
            p2[k // 2, k % 2] = acc.astype(BF16)
            acc = acc + r1[k].astype(F32)
        r2[chip] = p2[chip]

        def back(i, carry):
            k = lax.rem(chip + i, CHIPS)
            remote(p2.at[k], r2.at[chip], s2_s, s2_r, (2 * k, t)).start()
            return carry

        lax.fori_loop(1, CHIPS, back, 0)

    pltpu.make_async_copy(sb.at[0 : CHIPS - 1], sb.at[0 : CHIPS - 1], s1_s).wait()
    for d in (3, 1, 2):
        arrived(d, 1)
        local(d, 1)

    fwd = remote(r2, r2, s3_s, s3_r, (sib, t))

    @pl.when(core == 0)
    def _():
        pltpu.make_async_copy(p2.at[0 : CHIPS - 1], p2.at[0 : CHIPS - 1], s2_s).wait()
        pltpu.make_async_copy(r2.at[0 : CHIPS - 1], r2.at[0 : CHIPS - 1], s2_r).wait()
        fwd.start()

    @pl.when(core == 1)
    def _():
        fwd.wait_recv()

    pcopies = []
    for d in (1, 3, 2, 0):
        n = near(d)
        for k in range(CHIPS):
            h, o = k // 4, (k % 4) * ROWS
            val = (r2[k, core].astype(F32) + sc[2 * n, k * ROWS : (k + 1) * ROWS, :]).astype(BF16)
            if d:
                ps[d - 1, h, o : o + ROWS, :] = val
            else:
                pp[t, h, o : o + ROWS, :] = val
        if d:
            cp = remote(ps.at[d - 1], pp.at[t, :, 0:F, :], q_s.at[d - 1], q_r.at[d - 1], xpeer(d))
            cp.start()
            pcopies.append(cp)

    for d in (3, 1, 2):
        arrived(d, 0)
        local(d, 0)
        across(d)

    @pl.when(core == 0)
    def _():
        fwd.wait_send()

    for cp in wb:
        cp.wait()
    src = wf.at[1:4, :, :, core]
    wc = remote(src, src, wc_s, wc_r, (sib, t))
    wc.start()
    for cp in pcopies:
        cp.wait()

    results = []
    own = []
    for half in range(2):
        for d in range(TP):
            for h in range(HL):
                num = nl[half, d, :, h * DV : (h + 1) * DV] + jnp.dot(
                    fq[half, d, :, h * FP : (h + 1) * FP], pp[near(d), h], preferred_element_type=F32
                )
                spread_ = jnp.mean(num * num, axis=-1, keepdims=True)
                gh[half, d, :, h * DV : (h + 1) * DV] = (num * lax.rsqrt(spread_ + EPS)).astype(BF16)
        if half == 0:
            wocopy.wait()
            wc.wait()
        for n, d in enumerate((1, 3, 2, 0)):
            acc = jnp.zeros((C, 512), F32)
            for p in range(TP):
                acc = acc + jnp.dot(
                    gh[half, p], wf[d, near(p)].reshape(512, 512), preferred_element_type=F32
                )
            ob[half, n] = acc.astype(BF16)
            rows = out_ref.at[pl.ds(pl.multiple_of(t * 512 + half * C, C), C)]
            if d:
                cp = remote(ob.at[half, n], rows, b_s.at[half, d - 1], b_r.at[half, d - 1], xpeer(d))
                cp.start()
                results.append(cp)
            else:
                cp = pltpu.make_async_copy(ob.at[half, n], rows, own_s.at[half])
                cp.start()
                own.append(cp)

    for cp in sent + results:
        cp.wait_send()
    for half in range(2):
        for d in range(1, TP):
            rows = out_ref.at[pl.ds(pl.multiple_of(near(TP - d) * 512 + half * C, C), C)]
            remote(ob.at[half, 0], rows, b_s.at[half, 0], b_r.at[half, d - 1], xpeer(d)).wait_recv()
    for cp in own:
        cp.wait()


def body(tokens, gain, w_in, conv_taps, w_out):
    wt = jnp.transpose(w_in, (1, 2, 0)).reshape(HL * 160, D)
    eq, ek = feature_maps()
    hbm = pl.BlockSpec(memory_space=pl.ANY)
    vmem = pl.BlockSpec(memory_space=pltpu.VMEM)
    dma = pltpu.SemaphoreType.DMA
    width = VW + QW
    return pl.pallas_call(
        kernel,
        out_shape=jax.ShapeDtypeStruct((T, 512), BF16),
        in_specs=[hbm, vmem, hbm, vmem, hbm, hbm, hbm],
        out_specs=hbm,
        scratch_shapes=[
            pltpu.VMEM((NC, C, D), BF16),
            pltpu.VMEM((8 * NC, D), BF16),
            pltpu.VMEM((width, D), BF16),
            pltpu.VMEM((width, D), BF16),
            pltpu.VMEM((2, FP, HL * FP), BF16),
            pltpu.VMEM((2, HL * F, FP), BF16),
            pltpu.VMEM((8, width), F32),
            pltpu.VMEM((2, 8 + C, width), F32),
            pltpu.VMEM((8 + 8 * NC, width), F32),
            pltpu.VMEM((6, C, width), BF16),
            pltpu.VMEM((TP, 2, C, width), BF16),
            pltpu.VMEM((NC, HL * F, DV), F32),
            pltpu.VMEM((2, TP, C, VW), F32),
            pltpu.VMEM((2, TP, C, HL * FP), BF16),
            pltpu.VMEM((CHIPS, ROWS, DV), BF16),
            pltpu.VMEM((SEQ, ROWS, DV), BF16),
            pltpu.VMEM((CHIPS, 2, ROWS, DV), BF16),
            pltpu.VMEM((CHIPS, 2, ROWS, DV), BF16),
            pltpu.VMEM((3, HL, F, DV), BF16),
            pltpu.VMEM((TP, HL, FP, DV), BF16),
            pltpu.VMEM((4, 4, 4, 2, 64, 512), BF16),
            pltpu.VMEM((2, TP, C, VW), BF16),
            pltpu.VMEM((2, 4, C, 512), BF16),
            dma((3 + NC,)), dma((NC,)), dma, dma, dma, dma, dma, dma, dma, dma, dma,
            dma((3,)), dma((3,)), dma((6,)), dma((6,)), dma((6,)), dma((6,)), dma, dma,
            dma((2, 3)), dma((2, 3)), dma((3,)), dma((3,)), dma((2, 3)), dma((2, 3)), dma((2,)),
        ],
        compiler_params=pltpu.CompilerParams(
            collective_id=0, has_side_effects=True, vmem_limit_bytes=60 * 1024 * 1024
        ),
    )(
        tokens, gain.reshape(1, D), wt, conv_taps, w_out.reshape(4, 4, 2, 64, 512),
        jnp.asarray(eq), jnp.asarray(ek),
    )


def solution(mesh):
    return jax.shard_map(
        body,
        mesh=mesh,
        in_specs=(P("seq", None), P(), P(None, "tp", None), P(None, "tp", None), P(None, "tp")),
        out_specs=P("seq", "tp"),
        check_vma=False,
    )
```

```python
import functools
import math

import jax
import jax.numpy as jnp
import numpy as np
from jax import lax
from jax.experimental import pallas as pl
from jax.experimental.pallas import tpu as pltpu
from jax.sharding import PartitionSpec as P

DK = 16
DV = 128
HL = 4
T = 2048
D = 2048
C = 256
NC = T // C
F = 160
FP = 256
VW = HL * DV
QW = HL * 2 * DK
SEQ = 32
TP = 4
CHIPS = SEQ // 2
ROWS = HL * F // CHIPS
EPS = 1e-06
MESH = pl.DeviceIdType.MESH
F32 = jnp.float32
BF16 = jnp.bfloat16


def feature_maps():
    eq = np.zeros((2, FP, HL * FP), np.float32)
    ek = np.zeros((2, HL * F, FP), np.float32)
    one = QW
    for h in range(HL):
        q0, k0 = 2 * DK * h, 2 * DK * h + DK
        f = 0
        for i in range(DK):
            for j in range(i, DK):
                eq[0, q0 + i, h * FP + f] = (1.0 if i == j else 2.0) / 32.0
                eq[1, q0 + j, h * FP + f] = 1.0
                ek[0, h * F + f, k0 + i] = 1.0
                ek[1, h * F + f, k0 + j] = 1.0
                f += 1
        for i in range(DK):
            eq[0, q0 + i, h * FP + f] = 0.25
            eq[1, one, h * FP + f] = 1.0
            ek[0, h * F + f, k0 + i] = 1.0
            ek[1, h * F + f, one] = 1.0
            f += 1
        eq[0, one, h * FP + f] = 1.0
        eq[1, one, h * FP + f] = 1.0
        ek[0, h * F + f, one] = 1.0
        ek[1, h * F + f, one] = 1.0
    return eq.astype(jnp.bfloat16), ek.astype(jnp.bfloat16)


def kernel(
    x_hbm, gain_ref, wt_hbm, taps_ref, wo_hbm, eq_hbm, ek_hbm,
    out_ref,
    xv, xt8, wv, wg, eqv, ekv, taps, pf, tl, mx, ga, sc, nl, fq, sb, r1, p2, r2, ps, pp, wf, gh, ob,
    in_sem, x_sem, wo_sem, halo_s, halo_r, s1_s, s1_r, s2_s, s2_r, s3_s, s3_r,
    wx_s, wx_r, wa_s, wa_r, wb_s, wb_r, wc_s, wc_r, a_s, a_r, q_s, q_r, b_s, b_r, own_s,
):
    s = lax.axis_index("seq")
    t = lax.axis_index("tp")
    chip = s // 2
    core = s % 2
    zc = s // 8
    yc = (s // 2) % 4
    sib = s + 1 - 2 * core

    def remote(src, dst, ss, rs, dev):
        return pltpu.make_async_remote_copy(
            src_ref=src, dst_ref=dst, send_sem=ss, recv_sem=rs, device_id=dev, device_id_type=MESH
        )

    def near(d):
        return lax.rem(t + d, TP)

    def xpeer(d):
        return (s, near(d))

    def ypeer(d):
        return (zc * 8 + lax.rem(yc + d, 4) * 2 + core, t)

    def zpeer(d):
        return (lax.rem(zc + d, 4) * 8 + yc * 2 + core, t)

    tiles = [(d, half) for half in (1, 0) for d in (1, 3, 2)] + [(0, 1), (0, 0)]

    wcopy = pltpu.make_async_copy(wt_hbm, wv, in_sem.at[0])
    wcopy.start()
    tcopies = []
    for c in range(NC):
        cp = pltpu.make_async_copy(x_hbm.at[pl.ds(c * C + C - 8, 8)], xt8.at[pl.ds(8 * c, 8)], in_sem.at[3 + c])
        cp.start()
        tcopies.append(cp)
    xcopies = []
    for i, (d, half) in enumerate(tiles):
        base = pl.multiple_of((near(d) * 2 + half) * C, C)
        cp = pltpu.make_async_copy(x_hbm.at[pl.ds(base, C)], xv.at[i], x_sem.at[i])
        cp.start()
        xcopies.append(cp)
    ekcopy = pltpu.make_async_copy(ek_hbm, ekv, in_sem.at[1])
    ekcopy.start()
    eqcopy = pltpu.make_async_copy(eq_hbm, eqv, in_sem.at[2])
    eqcopy.start()
    wocopy = pltpu.make_async_copy(wo_hbm, wf.at[0], wo_sem)
    wocopy.start()

    barrier = pltpu.get_barrier_semaphore()

    def greet(j, carry):
        pl.semaphore_signal(barrier, inc=1, device_id=(lax.rem(s + j, SEQ), t), device_id_type=MESH)
        return carry

    lax.fori_loop(1, SEQ, greet, 0)
    for d in range(1, TP):
        pl.semaphore_signal(barrier, inc=1, device_id=xpeer(d), device_id_type=MESH)

    pp[:, :, F:, :] = jnp.zeros((TP, HL, FP - F, DV), BF16)

    row = lax.broadcasted_iota(jnp.int32, (160, 128), 0)
    col = lax.broadcasted_iota(jnp.int32, (160, 128), 1)
    pick_v = (row == col + 2 * DK).astype(F32).astype(BF16)
    for k in range(3):
        tk = taps_ref[k]
        tv = jnp.dot(tk, pick_v, preferred_element_type=F32)
        tq = jnp.zeros((1, QW), F32)
        for h in range(HL):
            taps[k : k + 1, h * DV : (h + 1) * DV] = tv[h : h + 1, :]
            pick_q = ((row + 2 * DK * h == col) & (row < 2 * DK)).astype(F32).astype(BF16)
            tq = tq + jnp.dot(tk, pick_q, preferred_element_type=F32)[h : h + 1, :]
        taps[k : k + 1, VW:] = tq

    wcopy.wait()
    gain = gain_ref[...].astype(F32)[None, :]
    for h in range(HL):
        for r in range(0, 160, 32):
            dst = VW + 32 * h if r == 0 else h * DV + r - 32
            src = h * 160 + r
            wg[dst : dst + 32, :] = (wv[src : src + 32, :].astype(F32) * gain).astype(BF16)

    def project(xt):
        xf = xt.astype(F32)
        scale = lax.rsqrt(jnp.mean(xf * xf, axis=-1, keepdims=True) + EPS)
        pr = lax.dot_general(xt, wg[...], (((1,), (1,)), ((), ())), preferred_element_type=F32)
        return (pr * scale).astype(BF16).astype(F32)

    for cp in tcopies:
        cp.wait()
    tl[8:, :] = project(xt8[...])

    pl.semaphore_wait(barrier, SEQ - 1 + TP - 1)
    halo = remote(tl.at[pl.ds(8 * NC, 8)], tl.at[pl.ds(0, 8)], halo_s, halo_r, (lax.rem(s + 1, SEQ), t))
    halo.start()
    wx = []
    for d in range(1, TP):
        cp = remote(
            wo_hbm.at[zc, yc, core], wf.at[TP - d, zc, yc, core], wx_s.at[d - 1], wx_r.at[d - 1], xpeer(d)
        )
        cp.start()
        wx.append(cp)

    def mix(i, c, dst):
        buf = pf.at[i % 2]
        buf[0:8, :] = tl[pl.ds(pl.multiple_of(c * 8, 8), 8), :]
        buf[8:, :] = project(xv[i])
        mixed = (
            buf[6 : 6 + C, :] * taps[0:1, :] + buf[7 : 7 + C, :] * taps[1:2, :] + buf[8 : 8 + C, :] * taps[2:3, :]
        )
        dst[...] = mixed.astype(BF16)

    def states(c, src):
        qe = jnp.concatenate(
            [jnp.transpose(src[:, VW:].astype(F32)).astype(BF16), jnp.ones((FP - QW, C), BF16)], axis=0
        )
        fk = (
            jnp.dot(ekv[0], qe, preferred_element_type=F32) * jnp.dot(ekv[1], qe, preferred_element_type=F32)
        ).astype(BF16)
        for h in range(HL):
            sc[c, h * F : (h + 1) * F, :] = jnp.dot(
                fk[h * F : (h + 1) * F, :], src[:, h * DV : (h + 1) * DV], preferred_element_type=F32
            )

    ekcopy.wait()
    sent = []
    wa = []
    wb = []
    for i, (d, half) in enumerate(tiles):
        c = near(d) * 2 + half
        if i == 3:
            halo.wait()
            tl[0:8, :] = jnp.where(s == 0, 0.0, tl[0:8, :])
        if i == 2:
            for cp in wx:
                cp.wait()
            for n in range(1, 4):
                src = wf.at[1:4, zc, yc, core, :, 0:256]
                cp = remote(src, src, wa_s.at[n - 1], wa_r.at[n - 1], ypeer(n))
                cp.start()
                wa.append(cp)
                src = wf.at[1:4, zc, yc, core, :, 256:512]
                cp = remote(src, src, wa_s.at[n + 2], wa_r.at[n + 2], zpeer(n))
                cp.start()
                wa.append(cp)
        if i == 6:
            for cp in wa:
                cp.wait()
            for n in range(1, 4):
                src = wf.at[1:4, zc, :, core, :, 0:256]
                cp = remote(src, src, wb_s.at[n - 1], wb_r.at[n - 1], zpeer(n))
                cp.start()
                wb.append(cp)
                src = wf.at[1:4, :, yc, core, :, 256:512]
                cp = remote(src, src, wb_s.at[n + 2], wb_r.at[n + 2], ypeer(n))
                cp.start()
                wb.append(cp)
        xcopies[i].wait()
        tile = mx.at[i] if d else ga.at[t, half]
        mix(i, c, tile)
        if d:
            cp = remote(tile, ga.at[t, half], a_s.at[half, d - 1], a_r.at[half, d - 1], xpeer(d))
            cp.start()
            sent.append(cp)
        states(c, tile)

    run = jnp.zeros((HL * F, DV), F32)
    for c in range(NC):
        part = sc[c]
        if c % 2 == 0:
            sc[c] = run
        run = run + part
    for k in range(CHIPS):
        sb[k] = run[k * ROWS : (k + 1) * ROWS, :].astype(BF16)

    def spread(i, carry):
        k = lax.rem(chip + i, CHIPS)
        remote(sb.at[k], r1.at[s], s1_s, s1_r, (2 * k, t)).start()
        return carry

    lax.fori_loop(1, CHIPS, spread, 0)

    @pl.when(core == 1)
    def _():
        remote(sb.at[chip], r1.at[s], s3_s, s1_r, (s - 1, t)).start()

    @pl.when(core == 0)
    def _():
        r1[s] = sb[chip]

    eqcopy.wait()
    pos = lax.broadcasted_iota(jnp.int32, (C, C), 0) >= lax.broadcasted_iota(jnp.int32, (C, C), 1)

    def arrived(d, half):
        n = TP - d - 1
        remote(mx.at[0], ga.at[near(d), half], a_s.at[half, n], a_r.at[half, n], xpeer(d)).wait_recv()

    def scores(q, kt, h):
        parts = []
        if h > 0:
            parts.append(jnp.zeros((32 * h, C), BF16))
        parts.append(kt[32 * h + 16 : 32 * h + 32, :])
        parts.append(jnp.zeros((QW - 32 * h - 16, C), BF16))
        up = jnp.dot(q, jnp.concatenate(parts, axis=0), preferred_element_type=F32) + 1.0
        return up * up * 0.5 + 0.5

    def keys(src):
        return (jnp.transpose(src[:, VW:].astype(F32)) * 0.25).astype(BF16)

    def local(d, half):
        src = ga.at[near(d), half]
        q = src[:, VW:]
        qe = jnp.concatenate([q, jnp.ones((C, FP - QW), BF16)], axis=1)
        kt = keys(src)
        for h in range(HL):
            fq[half, d, :, h * FP : (h + 1) * FP] = (
                jnp.dot(qe, eqv[0, :, h * FP : (h + 1) * FP], preferred_element_type=F32)
                * jnp.dot(qe, eqv[1, :, h * FP : (h + 1) * FP], preferred_element_type=F32)
            ).astype(BF16)
            w = jnp.where(pos, scores(q, kt, h), 0.0).astype(BF16)
            nl[half, d, :, h * DV : (h + 1) * DV] = jnp.dot(
                w, src[:, h * DV : (h + 1) * DV], preferred_element_type=F32
            )

    def across(d):
        q = ga[near(d), 1, :, VW:]
        src = ga.at[near(d), 0]
        kt = keys(src)
        for h in range(HL):
            w = scores(q, kt, h).astype(BF16)
            nl[1, d, :, h * DV : (h + 1) * DV] += jnp.dot(
                w, src[:, h * DV : (h + 1) * DV], preferred_element_type=F32
            )

    local(0, 1)
    local(0, 0)
    across(0)

    @pl.when(core == 0)
    def _():
        pltpu.make_async_copy(r1.at[0 : SEQ - 1], r1.at[0 : SEQ - 1], s1_r).wait()
        acc = jnp.zeros((ROWS, DV), F32)
        for k in range(SEQ):
            p2[k // 2, k % 2] = acc.astype(BF16)
            acc = acc + r1[k].astype(F32)
        r2[chip] = p2[chip]

        def back(i, carry):
            k = lax.rem(chip + i, CHIPS)
            remote(p2.at[k], r2.at[chip], s2_s, s2_r, (2 * k, t)).start()
            return carry

        lax.fori_loop(1, CHIPS, back, 0)

    pltpu.make_async_copy(sb.at[0 : CHIPS - 1], sb.at[0 : CHIPS - 1], s1_s).wait()
    for d in (3, 1, 2):
        arrived(d, 1)
        local(d, 1)

    fwd = remote(r2, r2, s3_s, s3_r, (sib, t))

    @pl.when(core == 0)
    def _():
        pltpu.make_async_copy(p2.at[0 : CHIPS - 1], p2.at[0 : CHIPS - 1], s2_s).wait()
        pltpu.make_async_copy(r2.at[0 : CHIPS - 1], r2.at[0 : CHIPS - 1], s2_r).wait()
        fwd.start()

    @pl.when(core == 1)
    def _():
        remote(sb.at[chip], r1.at[s], s3_s, s1_r, (s - 1, t)).wait_send()
        fwd.wait_recv()

    pcopies = []
    for d in (1, 3, 2, 0):
        n = near(d)
        for k in range(CHIPS):
            h, o = k // 4, (k % 4) * ROWS
            val = (r2[k, core].astype(F32) + sc[2 * n, k * ROWS : (k + 1) * ROWS, :]).astype(BF16)
            if d:
                ps[d - 1, h, o : o + ROWS, :] = val
            else:
                pp[t, h, o : o + ROWS, :] = val
        if d:
            cp = remote(ps.at[d - 1], pp.at[t, :, 0:F, :], q_s.at[d - 1], q_r.at[d - 1], xpeer(d))
            cp.start()
            pcopies.append(cp)

    for d in (3, 1, 2):
        arrived(d, 0)
        local(d, 0)
        across(d)

    @pl.when(core == 0)
    def _():
        fwd.wait_send()

    for cp in wb:
        cp.wait()
    src = wf.at[1:4, :, :, core]
    wc = remote(src, src, wc_s, wc_r, (sib, t))
    wc.start()
    for cp in pcopies:
        cp.wait()

    results = []
    own = []
    for half in range(2):
        for d in range(TP):
            for h in range(HL):
                num = nl[half, d, :, h * DV : (h + 1) * DV] + jnp.dot(
                    fq[half, d, :, h * FP : (h + 1) * FP], pp[near(d), h], preferred_element_type=F32
                )
                spread_ = jnp.mean(num * num, axis=-1, keepdims=True)
                gh[half, d, :, h * DV : (h + 1) * DV] = (num * lax.rsqrt(spread_ + EPS)).astype(BF16)
        if half == 0:
            wocopy.wait()
            wc.wait()
        for n, d in enumerate((1, 3, 2, 0)):
            acc = jnp.zeros((C, 512), F32)
            for p in range(TP):
                acc = acc + jnp.dot(
                    gh[half, p], wf[d, near(p)].reshape(512, 512), preferred_element_type=F32
                )
            ob[half, n] = acc.astype(BF16)
            rows = out_ref.at[pl.ds(pl.multiple_of(t * 512 + half * C, C), C)]
            if d:
                cp = remote(ob.at[half, n], rows, b_s.at[half, d - 1], b_r.at[half, d - 1], xpeer(d))
                cp.start()
                results.append(cp)
            else:
                cp = pltpu.make_async_copy(ob.at[half, n], rows, own_s.at[half])
                cp.start()
                own.append(cp)

    for cp in sent + results:
        cp.wait_send()
    for half in range(2):
        for d in range(1, TP):
            rows = out_ref.at[pl.ds(pl.multiple_of(near(TP - d) * 512 + half * C, C), C)]
            remote(ob.at[half, 0], rows, b_s.at[half, 0], b_r.at[half, d - 1], xpeer(d)).wait_recv()
    for cp in own:
        cp.wait()


def body(tokens, gain, w_in, conv_taps, w_out):
    wt = jnp.transpose(w_in, (1, 2, 0)).reshape(HL * 160, D)
    eq, ek = feature_maps()
    hbm = pl.BlockSpec(memory_space=pl.ANY)
    vmem = pl.BlockSpec(memory_space=pltpu.VMEM)
    dma = pltpu.SemaphoreType.DMA
    width = VW + QW
    return pl.pallas_call(
        kernel,
        out_shape=jax.ShapeDtypeStruct((T, 512), BF16),
        in_specs=[hbm, vmem, hbm, vmem, hbm, hbm, hbm],
        out_specs=hbm,
        scratch_shapes=[
            pltpu.VMEM((NC, C, D), BF16),
            pltpu.VMEM((8 * NC, D), BF16),
            pltpu.VMEM((width, D), BF16),
            pltpu.VMEM((width, D), BF16),
            pltpu.VMEM((2, FP, HL * FP), BF16),
            pltpu.VMEM((2, HL * F, FP), BF16),
            pltpu.VMEM((8, width), F32),
            pltpu.VMEM((2, 8 + C, width), F32),
            pltpu.VMEM((8 + 8 * NC, width), F32),
            pltpu.VMEM((6, C, width), BF16),
            pltpu.VMEM((TP, 2, C, width), BF16),
            pltpu.VMEM((NC, HL * F, DV), F32),
            pltpu.VMEM((2, TP, C, VW), F32),
            pltpu.VMEM((2, TP, C, HL * FP), BF16),
            pltpu.VMEM((CHIPS, ROWS, DV), BF16),
            pltpu.VMEM((SEQ, ROWS, DV), BF16),
            pltpu.VMEM((CHIPS, 2, ROWS, DV), BF16),
            pltpu.VMEM((CHIPS, 2, ROWS, DV), BF16),
            pltpu.VMEM((3, HL, F, DV), BF16),
            pltpu.VMEM((TP, HL, FP, DV), BF16),
            pltpu.VMEM((4, 4, 4, 2, 64, 512), BF16),
            pltpu.VMEM((2, TP, C, VW), BF16),
            pltpu.VMEM((2, 4, C, 512), BF16),
            dma((3 + NC,)), dma((NC,)), dma, dma, dma, dma, dma, dma, dma, dma, dma,
            dma((3,)), dma((3,)), dma((6,)), dma((6,)), dma((6,)), dma((6,)), dma, dma,
            dma((2, 3)), dma((2, 3)), dma((3,)), dma((3,)), dma((2, 3)), dma((2, 3)), dma((2,)),
        ],
        compiler_params=pltpu.CompilerParams(
            collective_id=0, has_side_effects=True, vmem_limit_bytes=50 * 1024 * 1024
        ),
    )(
        tokens, gain, wt, conv_taps, w_out.reshape(4, 4, 2, 64, 512),
        jnp.asarray(eq), jnp.asarray(ek),
    )


def solution(mesh):
    return jax.shard_map(
        body,
        mesh=mesh,
        in_specs=(P("seq", None), P(), P(None, "tp", None), P(None, "tp", None), P(None, "tp")),
        out_specs=P("seq", "tp"),
        check_vma=False,
    )
```

```python
import functools
import math

import jax
import jax.numpy as jnp
import numpy as np
from jax import lax
from jax.experimental import pallas as pl
from jax.experimental.pallas import tpu as pltpu
from jax.sharding import PartitionSpec as P

DK = 16
DV = 128
HL = 4
T = 2048
D = 2048
C = 256
NC = T // C
F = 160
FP = 256
VW = HL * DV
QW = HL * 2 * DK
SEQ = 32
TP = 4
CHIPS = SEQ // 2
ROWS = HL * F // CHIPS
EPS = 1e-06
MESH = pl.DeviceIdType.MESH
F32 = jnp.float32
BF16 = jnp.bfloat16


def feature_maps():
    eq = np.zeros((2, FP, HL * FP), np.float32)
    ek = np.zeros((2, HL * F, FP), np.float32)
    one = QW
    for h in range(HL):
        q0, k0 = 2 * DK * h, 2 * DK * h + DK
        f = 0
        for i in range(DK):
            for j in range(i, DK):
                eq[0, q0 + i, h * FP + f] = (1.0 if i == j else 2.0) / 32.0
                eq[1, q0 + j, h * FP + f] = 1.0
                ek[0, h * F + f, k0 + i] = 1.0
                ek[1, h * F + f, k0 + j] = 1.0
                f += 1
        for i in range(DK):
            eq[0, q0 + i, h * FP + f] = 0.25
            eq[1, one, h * FP + f] = 1.0
            ek[0, h * F + f, k0 + i] = 1.0
            ek[1, h * F + f, one] = 1.0
            f += 1
        eq[0, one, h * FP + f] = 1.0
        eq[1, one, h * FP + f] = 1.0
        ek[0, h * F + f, one] = 1.0
        ek[1, h * F + f, one] = 1.0
    return eq.astype(jnp.bfloat16), ek.astype(jnp.bfloat16)


def kernel(
    x_hbm, gain_ref, wt_hbm, taps_ref, wo_hbm, eq_hbm, ek_hbm,
    out_ref,
    xv, xt8, wv, wg, eqv, ekv, taps, pf, tl, mx, ga, sc, nl, fq, sb, r1, p2, r2, ps, pp, wf, gh, ob,
    in_sem, x_sem, wo_sem, halo_s, halo_r, s1_s, s1_r, s2_s, s2_r, s3_s, s3_r,
    wx_s, wx_r, wa_s, wa_r, wb_s, wb_r, wc_s, wc_r, a_s, a_r, q_s, q_r, b_s, b_r, own_s,
):
    s = lax.axis_index("seq")
    t = lax.axis_index("tp")
    chip = s // 2
    core = s % 2
    zc = s // 8
    yc = (s // 2) % 4
    sib = s + 1 - 2 * core

    def remote(src, dst, ss, rs, dev):
        return pltpu.make_async_remote_copy(
            src_ref=src, dst_ref=dst, send_sem=ss, recv_sem=rs, device_id=dev, device_id_type=MESH
        )

    def near(d):
        return lax.rem(t + d, TP)

    def xpeer(d):
        return (s, near(d))

    def ypeer(d):
        return (zc * 8 + lax.rem(yc + d, 4) * 2 + core, t)

    def zpeer(d):
        return (lax.rem(zc + d, 4) * 8 + yc * 2 + core, t)

    tiles = [(d, half) for half in (1, 0) for d in (1, 3, 2)] + [(0, 1), (0, 0)]

    wcopy = pltpu.make_async_copy(wt_hbm, wv, in_sem.at[0])
    wcopy.start()
    tcopies = []
    for c in range(NC):
        cp = pltpu.make_async_copy(x_hbm.at[pl.ds(c * C + C - 8, 8)], xt8.at[pl.ds(8 * c, 8)], in_sem.at[3 + c])
        cp.start()
        tcopies.append(cp)
    xcopies = []
    for i, (d, half) in enumerate(tiles):
        base = pl.multiple_of((near(d) * 2 + half) * C, C)
        cp = pltpu.make_async_copy(x_hbm.at[pl.ds(base, C)], xv.at[i], x_sem.at[i])
        cp.start()
        xcopies.append(cp)
    ekcopy = pltpu.make_async_copy(ek_hbm, ekv, in_sem.at[1])
    ekcopy.start()
    eqcopy = pltpu.make_async_copy(eq_hbm, eqv, in_sem.at[2])
    eqcopy.start()
    wocopy = pltpu.make_async_copy(wo_hbm, wf.at[0], wo_sem)
    wocopy.start()

    barrier = pltpu.get_barrier_semaphore()

    def greet(j, carry):
        pl.semaphore_signal(barrier, inc=1, device_id=(lax.rem(s + j, SEQ), t), device_id_type=MESH)
        return carry

    lax.fori_loop(1, SEQ, greet, 0)
    for d in range(1, TP):
        pl.semaphore_signal(barrier, inc=1, device_id=xpeer(d), device_id_type=MESH)

    pp[:, :, F:, :] = jnp.zeros((TP, HL, FP - F, DV), BF16)

    row = lax.broadcasted_iota(jnp.int32, (160, 128), 0)
    col = lax.broadcasted_iota(jnp.int32, (160, 128), 1)
    pick_v = (row == col + 2 * DK).astype(F32).astype(BF16)
    for k in range(3):
        tk = taps_ref[k]
        tv = jnp.dot(tk, pick_v, preferred_element_type=F32)
        tq = jnp.zeros((1, QW), F32)
        for h in range(HL):
            taps[k : k + 1, h * DV : (h + 1) * DV] = tv[h : h + 1, :]
            pick_q = ((row + 2 * DK * h == col) & (row < 2 * DK)).astype(F32).astype(BF16)
            tq = tq + jnp.dot(tk, pick_q, preferred_element_type=F32)[h : h + 1, :]
        taps[k : k + 1, VW:] = tq

    wcopy.wait()
    gain = gain_ref[...].astype(F32)[None, :]
    for h in range(HL):
        for r in range(0, 160, 32):
            dst = VW + 32 * h if r == 0 else h * DV + r - 32
            src = h * 160 + r
            wg[dst : dst + 32, :] = (wv[src : src + 32, :].astype(F32) * gain).astype(BF16)

    def project(xt):
        xf = xt.astype(F32)
        scale = lax.rsqrt(jnp.mean(xf * xf, axis=-1, keepdims=True) + EPS)
        pr = lax.dot_general(xt, wg[...], (((1,), (1,)), ((), ())), preferred_element_type=F32)
        return (pr * scale).astype(BF16).astype(F32)

    for cp in tcopies:
        cp.wait()
    tl[8:, :] = project(xt8[...])

    pl.semaphore_wait(barrier, SEQ - 1 + TP - 1)
    halo = remote(tl.at[pl.ds(8 * NC, 8)], tl.at[pl.ds(0, 8)], halo_s, halo_r, (lax.rem(s + 1, SEQ), t))
    halo.start()
    wx = []
    for d in range(1, TP):
        cp = remote(
            wo_hbm.at[zc, yc, core], wf.at[TP - d, zc, yc, core], wx_s.at[d - 1], wx_r.at[d - 1], xpeer(d)
        )
        cp.start()
        wx.append(cp)

    def mix(i, c, dst):
        buf = pf.at[i % 2]
        buf[0:8, :] = tl[pl.ds(pl.multiple_of(c * 8, 8), 8), :]
        buf[8:, :] = project(xv[i])
        mixed = (
            buf[6 : 6 + C, :] * taps[0:1, :] + buf[7 : 7 + C, :] * taps[1:2, :] + buf[8 : 8 + C, :] * taps[2:3, :]
        )
        dst[...] = mixed.astype(BF16)

    def states(c, src):
        qe = jnp.concatenate(
            [jnp.transpose(src[:, VW:].astype(F32)).astype(BF16), jnp.ones((FP - QW, C), BF16)], axis=0
        )
        fk = (
            jnp.dot(ekv[0], qe, preferred_element_type=F32) * jnp.dot(ekv[1], qe, preferred_element_type=F32)
        ).astype(BF16)
        for h in range(HL):
            sc[c, h * F : (h + 1) * F, :] = jnp.dot(
                fk[h * F : (h + 1) * F, :], src[:, h * DV : (h + 1) * DV], preferred_element_type=F32
            )

    sent = []
    wa = []
    wb = {1: [], 2: [], 3: []}

    def onward(shard):
        n = 6 * (shard - 1)
        for d in range(1, 4):
            src = wf.at[shard, zc, :, core, :, 0:256]
            cp = remote(src, src, wb_s.at[n], wb_r.at[n], zpeer(d))
            cp.start()
            wb[shard].append(cp)
            src = wf.at[shard, :, yc, core, :, 256:512]
            cp = remote(src, src, wb_s.at[n + 1], wb_r.at[n + 1], ypeer(d))
            cp.start()
            wb[shard].append(cp)
            n += 2

    def across_cores(shard):
        for cp in wb[shard]:
            cp.wait()
        src = wf.at[shard, :, :, core]
        cp = remote(src, src, wc_s.at[shard - 1], wc_r.at[shard - 1], (sib, t))
        cp.start()
        return cp

    ekcopy.wait()
    for i, (d, half) in enumerate(tiles):
        c = near(d) * 2 + half
        if i == 3:
            halo.wait()
            tl[0:8, :] = jnp.where(s == 0, 0.0, tl[0:8, :])
        if i == 2:
            for cp in wx:
                cp.wait()
            for n in range(1, 4):
                src = wf.at[1:4, zc, yc, core, :, 0:256]
                cp = remote(src, src, wa_s.at[n - 1], wa_r.at[n - 1], ypeer(n))
                cp.start()
                wa.append(cp)
                src = wf.at[1:4, zc, yc, core, :, 256:512]
                cp = remote(src, src, wa_s.at[n + 2], wa_r.at[n + 2], zpeer(n))
                cp.start()
                wa.append(cp)
        if i == 5:
            for cp in wa:
                cp.wait()
            onward(1)
        xcopies[i].wait()
        tile = mx.at[i] if d else ga.at[t, half]
        mix(i, c, tile)
        if d:
            cp = remote(tile, ga.at[t, half], a_s.at[half, d - 1], a_r.at[half, d - 1], xpeer(d))
            cp.start()
            sent.append(cp)
        states(c, tile)

    run = jnp.zeros((HL * F, DV), F32)
    for c in range(NC):
        part = sc[c]
        if c % 2 == 0:
            sc[c] = run
        run = run + part
    for k in range(CHIPS):
        sb[k] = run[k * ROWS : (k + 1) * ROWS, :].astype(BF16)

    def spread(i, carry):
        k = lax.rem(chip + i, CHIPS)
        remote(sb.at[k], r1.at[s], s1_s, s1_r, (2 * k, t)).start()
        return carry

    lax.fori_loop(1, CHIPS, spread, 0)

    @pl.when(core == 1)
    def _():
        remote(sb.at[chip], r1.at[s], s3_s, s1_r, (s - 1, t)).start()

    @pl.when(core == 0)
    def _():
        r1[s] = sb[chip]

    eqcopy.wait()
    pos = lax.broadcasted_iota(jnp.int32, (C, C), 0) >= lax.broadcasted_iota(jnp.int32, (C, C), 1)

    def arrived(d, half):
        n = TP - d - 1
        remote(mx.at[0], ga.at[near(d), half], a_s.at[half, n], a_r.at[half, n], xpeer(d)).wait_recv()

    def scores(q, kt, h):
        parts = []
        if h > 0:
            parts.append(jnp.zeros((32 * h, C), BF16))
        parts.append(kt[32 * h + 16 : 32 * h + 32, :])
        parts.append(jnp.zeros((QW - 32 * h - 16, C), BF16))
        up = jnp.dot(q, jnp.concatenate(parts, axis=0), preferred_element_type=F32) + 1.0
        return up * up * 0.5 + 0.5

    def keys(src):
        return (jnp.transpose(src[:, VW:].astype(F32)) * 0.25).astype(BF16)

    def local(d, half):
        src = ga.at[near(d), half]
        q = src[:, VW:]
        qe = jnp.concatenate([q, jnp.ones((C, FP - QW), BF16)], axis=1)
        kt = keys(src)
        for h in range(HL):
            fq[half, d, :, h * FP : (h + 1) * FP] = (
                jnp.dot(qe, eqv[0, :, h * FP : (h + 1) * FP], preferred_element_type=F32)
                * jnp.dot(qe, eqv[1, :, h * FP : (h + 1) * FP], preferred_element_type=F32)
            ).astype(BF16)
            w = jnp.where(pos, scores(q, kt, h), 0.0).astype(BF16)
            nl[half, d, :, h * DV : (h + 1) * DV] = jnp.dot(
                w, src[:, h * DV : (h + 1) * DV], preferred_element_type=F32
            )

    def across(d):
        q = ga[near(d), 1, :, VW:]
        src = ga.at[near(d), 0]
        kt = keys(src)
        for h in range(HL):
            w = scores(q, kt, h).astype(BF16)
            nl[1, d, :, h * DV : (h + 1) * DV] += jnp.dot(
                w, src[:, h * DV : (h + 1) * DV], preferred_element_type=F32
            )

    local(0, 1)
    local(0, 0)
    across(0)

    @pl.when(core == 0)
    def _():
        pltpu.make_async_copy(r1.at[0 : SEQ - 1], r1.at[0 : SEQ - 1], s1_r).wait()
        acc = jnp.zeros((ROWS, DV), F32)
        for k in range(SEQ):
            p2[k // 2, k % 2] = acc.astype(BF16)
            acc = acc + r1[k].astype(F32)
        r2[chip] = p2[chip]

        def back(i, carry):
            k = lax.rem(chip + i, CHIPS)
            remote(p2.at[k], r2.at[chip], s2_s, s2_r, (2 * k, t)).start()
            return carry

        lax.fori_loop(1, CHIPS, back, 0)

    pltpu.make_async_copy(sb.at[0 : CHIPS - 1], sb.at[0 : CHIPS - 1], s1_s).wait()
    for d in (3, 1, 2):
        arrived(d, 1)
        local(d, 1)

    fwd = remote(r2, r2, s3_s, s3_r, (sib, t))

    @pl.when(core == 0)
    def _():
        pltpu.make_async_copy(p2.at[0 : CHIPS - 1], p2.at[0 : CHIPS - 1], s2_s).wait()
        pltpu.make_async_copy(r2.at[0 : CHIPS - 1], r2.at[0 : CHIPS - 1], s2_r).wait()
        fwd.start()

    @pl.when(core == 1)
    def _():
        remote(sb.at[chip], r1.at[s], s3_s, s1_r, (s - 1, t)).wait_send()
        fwd.wait_recv()

    pcopies = []
    for d in (1, 3, 2, 0):
        n = near(d)
        for k in range(CHIPS):
            h, o = k // 4, (k % 4) * ROWS
            val = (r2[k, core].astype(F32) + sc[2 * n, k * ROWS : (k + 1) * ROWS, :]).astype(BF16)
            if d:
                ps[d - 1, h, o : o + ROWS, :] = val
            else:
                pp[t, h, o : o + ROWS, :] = val
        if d:
            cp = remote(ps.at[d - 1], pp.at[t, :, 0:F, :], q_s.at[d - 1], q_r.at[d - 1], xpeer(d))
            cp.start()
            pcopies.append(cp)
    wc = {1: across_cores(1)}
    onward(3)
    onward(2)

    for d in (3, 1, 2):
        arrived(d, 0)
        local(d, 0)
        across(d)

    @pl.when(core == 0)
    def _():
        fwd.wait_send()

    for cp in pcopies:
        cp.wait()

    results = []
    own = []
    for half in range(2):
        for d in range(TP):
            for h in range(HL):
                num = nl[half, d, :, h * DV : (h + 1) * DV] + jnp.dot(
                    fq[half, d, :, h * FP : (h + 1) * FP], pp[near(d), h], preferred_element_type=F32
                )
                spread_ = jnp.mean(num * num, axis=-1, keepdims=True)
                gh[half, d, :, h * DV : (h + 1) * DV] = (num * lax.rsqrt(spread_ + EPS)).astype(BF16)
        for n, d in enumerate((1, 3, 2, 0)):
            if half == 0:
                if d:
                    wc[d].wait()
                else:
                    wocopy.wait()
            if half == 0 and n == 0:
                wc[3] = across_cores(3)
            if half == 0 and n == 1:
                wc[2] = across_cores(2)
            acc = jnp.zeros((C, 512), F32)
            for p in range(TP):
                acc = acc + jnp.dot(
                    gh[half, p], wf[d, near(p)].reshape(512, 512), preferred_element_type=F32
                )
            ob[half, n] = acc.astype(BF16)
            rows = out_ref.at[pl.ds(pl.multiple_of(t * 512 + half * C, C), C)]
            if d:
                cp = remote(ob.at[half, n], rows, b_s.at[half, d - 1], b_r.at[half, d - 1], xpeer(d))
                cp.start()
                results.append(cp)
            else:
                cp = pltpu.make_async_copy(ob.at[half, n], rows, own_s.at[half])
                cp.start()
                own.append(cp)

    for cp in sent + results:
        cp.wait_send()
    for half in range(2):
        for d in range(1, TP):
            rows = out_ref.at[pl.ds(pl.multiple_of(near(TP - d) * 512 + half * C, C), C)]
            remote(ob.at[half, 0], rows, b_s.at[half, 0], b_r.at[half, d - 1], xpeer(d)).wait_recv()
    for cp in own:
        cp.wait()


def body(tokens, gain, w_in, conv_taps, w_out):
    wt = jnp.transpose(w_in, (1, 2, 0)).reshape(HL * 160, D)
    eq, ek = feature_maps()
    hbm = pl.BlockSpec(memory_space=pl.ANY)
    vmem = pl.BlockSpec(memory_space=pltpu.VMEM)
    dma = pltpu.SemaphoreType.DMA
    width = VW + QW
    return pl.pallas_call(
        kernel,
        out_shape=jax.ShapeDtypeStruct((T, 512), BF16),
        in_specs=[hbm, vmem, hbm, vmem, hbm, hbm, hbm],
        out_specs=hbm,
        scratch_shapes=[
            pltpu.VMEM((NC, C, D), BF16),
            pltpu.VMEM((8 * NC, D), BF16),
            pltpu.VMEM((width, D), BF16),
            pltpu.VMEM((width, D), BF16),
            pltpu.VMEM((2, FP, HL * FP), BF16),
            pltpu.VMEM((2, HL * F, FP), BF16),
            pltpu.VMEM((8, width), F32),
            pltpu.VMEM((2, 8 + C, width), F32),
            pltpu.VMEM((8 + 8 * NC, width), F32),
            pltpu.VMEM((6, C, width), BF16),
            pltpu.VMEM((TP, 2, C, width), BF16),
            pltpu.VMEM((NC, HL * F, DV), F32),
            pltpu.VMEM((2, TP, C, VW), F32),
            pltpu.VMEM((2, TP, C, HL * FP), BF16),
            pltpu.VMEM((CHIPS, ROWS, DV), BF16),
            pltpu.VMEM((SEQ, ROWS, DV), BF16),
            pltpu.VMEM((CHIPS, 2, ROWS, DV), BF16),
            pltpu.VMEM((CHIPS, 2, ROWS, DV), BF16),
            pltpu.VMEM((3, HL, F, DV), BF16),
            pltpu.VMEM((TP, HL, FP, DV), BF16),
            pltpu.VMEM((4, 4, 4, 2, 64, 512), BF16),
            pltpu.VMEM((2, TP, C, VW), BF16),
            pltpu.VMEM((2, 4, C, 512), BF16),
            dma((3 + NC,)), dma((NC,)), dma, dma, dma, dma, dma, dma, dma, dma, dma,
            dma((3,)), dma((3,)), dma((6,)), dma((6,)), dma((18,)), dma((18,)), dma((3,)), dma((3,)),
            dma((2, 3)), dma((2, 3)), dma((3,)), dma((3,)), dma((2, 3)), dma((2, 3)), dma((2,)),
        ],
        compiler_params=pltpu.CompilerParams(
            collective_id=0, has_side_effects=True, vmem_limit_bytes=59 * 1024 * 1024
        ),
    )(
        tokens, gain, wt, conv_taps, w_out.reshape(4, 4, 2, 64, 512),
        jnp.asarray(eq), jnp.asarray(ek),
    )


def solution(mesh):
    return jax.shard_map(
        body,
        mesh=mesh,
        in_specs=(P("seq", None), P(), P(None, "tp", None), P(None, "tp", None), P(None, "tp")),
        out_specs=P("seq", "tp"),
        check_vma=False,
    )
```

```python
import functools
import math

import jax
import jax.numpy as jnp
import numpy as np
from jax import lax
from jax.experimental import pallas as pl
from jax.experimental.pallas import tpu as pltpu
from jax.sharding import PartitionSpec as P

DK = 16
DV = 128
HL = 4
T = 2048
D = 2048
C = 256
NC = T // C
F = 160
FP = 256
VW = HL * DV
QW = HL * 2 * DK
SEQ = 32
TP = 4
CHIPS = SEQ // 2
ROWS = HL * F // CHIPS
EPS = 1e-06
MESH = pl.DeviceIdType.MESH
F32 = jnp.float32
BF16 = jnp.bfloat16


def feature_maps():
    eq = np.zeros((2, FP, HL * FP), np.float32)
    ek = np.zeros((2, HL * F, FP), np.float32)
    one = QW
    for h in range(HL):
        q0, k0 = 2 * DK * h, 2 * DK * h + DK
        f = 0
        for i in range(DK):
            for j in range(i, DK):
                eq[0, q0 + i, h * FP + f] = (1.0 if i == j else 2.0) / 32.0
                eq[1, q0 + j, h * FP + f] = 1.0
                ek[0, h * F + f, k0 + i] = 1.0
                ek[1, h * F + f, k0 + j] = 1.0
                f += 1
        for i in range(DK):
            eq[0, q0 + i, h * FP + f] = 0.25
            eq[1, one, h * FP + f] = 1.0
            ek[0, h * F + f, k0 + i] = 1.0
            ek[1, h * F + f, one] = 1.0
            f += 1
        eq[0, one, h * FP + f] = 1.0
        eq[1, one, h * FP + f] = 1.0
        ek[0, h * F + f, one] = 1.0
        ek[1, h * F + f, one] = 1.0
    return eq.astype(jnp.bfloat16), ek.astype(jnp.bfloat16)


def kernel(
    x_hbm, gain_ref, wt_hbm, taps_ref, wo_hbm, eq_hbm, ek_hbm,
    out_ref,
    xv, xt8, wv, wg, eqv, ekv, taps, pf, tl, mx, ga, sc, nl, fq, sb, r1, p2, r2, ps, pp, wf, gh, ob,
    in_sem, w_sem, x_sem, wo_sem, halo_s, halo_r, s1_s, s1_r, s2_s, s2_r, s3_s, s3_r,
    wx_s, wx_r, wa_s, wa_r, wb_s, wb_r, wc_s, wc_r, a_s, a_r, q_s, q_r, b_s, b_r, own_s,
):
    s = lax.axis_index("seq")
    t = lax.axis_index("tp")
    chip = s // 2
    core = s % 2
    zc = s // 8
    yc = (s // 2) % 4
    sib = s + 1 - 2 * core

    def remote(src, dst, ss, rs, dev):
        return pltpu.make_async_remote_copy(
            src_ref=src, dst_ref=dst, send_sem=ss, recv_sem=rs, device_id=dev, device_id_type=MESH
        )

    def near(d):
        return lax.rem(t + d, TP)

    def xpeer(d):
        return (s, near(d))

    def ypeer(d):
        return (zc * 8 + lax.rem(yc + d, 4) * 2 + core, t)

    def zpeer(d):
        return (lax.rem(zc + d, 4) * 8 + yc * 2 + core, t)

    tiles = [(d, half) for half in (1, 0) for d in (1, 3, 2)] + [(0, 1), (0, 0)]

    wcopies = []
    for h in range(HL):
        rows = pl.ds(160 * h, 160)
        cp = pltpu.make_async_copy(wt_hbm.at[rows], wv.at[rows], w_sem.at[h])
        cp.start()
        wcopies.append(cp)
    tcopies = []
    for c in range(NC):
        cp = pltpu.make_async_copy(x_hbm.at[pl.ds(c * C + C - 8, 8)], xt8.at[pl.ds(8 * c, 8)], in_sem.at[3 + c])
        cp.start()
        tcopies.append(cp)
    xcopies = []
    for i, (d, half) in enumerate(tiles):
        base = pl.multiple_of((near(d) * 2 + half) * C, C)
        cp = pltpu.make_async_copy(x_hbm.at[pl.ds(base, C)], xv.at[i], x_sem.at[i])
        cp.start()
        xcopies.append(cp)
    ekcopy = pltpu.make_async_copy(ek_hbm, ekv, in_sem.at[1])
    ekcopy.start()
    eqcopy = pltpu.make_async_copy(eq_hbm, eqv, in_sem.at[2])
    eqcopy.start()
    wocopy = pltpu.make_async_copy(wo_hbm, wf.at[0], wo_sem)
    wocopy.start()

    barrier = pltpu.get_barrier_semaphore()

    def greet(j, carry):
        pl.semaphore_signal(barrier, inc=1, device_id=(lax.rem(s + j, SEQ), t), device_id_type=MESH)
        return carry

    lax.fori_loop(1, SEQ, greet, 0)
    for d in range(1, TP):
        pl.semaphore_signal(barrier, inc=1, device_id=xpeer(d), device_id_type=MESH)

    pp[:, :, F:, :] = jnp.zeros((TP, HL, FP - F, DV), BF16)

    row = lax.broadcasted_iota(jnp.int32, (160, 128), 0)
    col = lax.broadcasted_iota(jnp.int32, (160, 128), 1)
    pick_v = (row == col + 2 * DK).astype(F32).astype(BF16)
    for k in range(3):
        tk = taps_ref[k]
        tv = jnp.dot(tk, pick_v, preferred_element_type=F32)
        tq = jnp.zeros((1, QW), F32)
        for h in range(HL):
            taps[k : k + 1, h * DV : (h + 1) * DV] = tv[h : h + 1, :]
            pick_q = ((row + 2 * DK * h == col) & (row < 2 * DK)).astype(F32).astype(BF16)
            tq = tq + jnp.dot(tk, pick_q, preferred_element_type=F32)[h : h + 1, :]
        taps[k : k + 1, VW:] = tq

    gain = gain_ref[...].astype(F32)[None, :]
    for h in range(HL):
        wcopies[h].wait()
        for r in range(0, 160, 32):
            dst = VW + 32 * h if r == 0 else h * DV + r - 32
            src = h * 160 + r
            wg[dst : dst + 32, :] = (wv[src : src + 32, :].astype(F32) * gain).astype(BF16)

    def project(xt):
        xf = xt.astype(F32)
        scale = lax.rsqrt(jnp.mean(xf * xf, axis=-1, keepdims=True) + EPS)
        pr = lax.dot_general(xt, wg[...], (((1,), (1,)), ((), ())), preferred_element_type=F32)
        return (pr * scale).astype(BF16).astype(F32)

    for cp in tcopies:
        cp.wait()
    tl[8:, :] = project(xt8[...])

    pl.semaphore_wait(barrier, SEQ - 1 + TP - 1)
    halo = remote(tl.at[pl.ds(8 * NC, 8)], tl.at[pl.ds(0, 8)], halo_s, halo_r, (lax.rem(s + 1, SEQ), t))
    halo.start()
    wx = []
    for d in range(1, TP):
        cp = remote(
            wo_hbm.at[zc, yc, core], wf.at[TP - d, zc, yc, core], wx_s.at[d - 1], wx_r.at[d - 1], xpeer(d)
        )
        cp.start()
        wx.append(cp)

    def mix(i, c, dst):
        buf = pf.at[i % 2]
        buf[0:8, :] = tl[pl.ds(pl.multiple_of(c * 8, 8), 8), :]
        buf[8:, :] = project(xv[i])
        mixed = (
            buf[6 : 6 + C, :] * taps[0:1, :] + buf[7 : 7 + C, :] * taps[1:2, :] + buf[8 : 8 + C, :] * taps[2:3, :]
        )
        dst[...] = mixed.astype(BF16)

    def states(c, src):
        qe = jnp.concatenate(
            [jnp.transpose(src[:, VW:].astype(F32)).astype(BF16), jnp.ones((FP - QW, C), BF16)], axis=0
        )
        fk = (
            jnp.dot(ekv[0], qe, preferred_element_type=F32) * jnp.dot(ekv[1], qe, preferred_element_type=F32)
        ).astype(BF16)
        for h in range(HL):
            sc[c, h * F : (h + 1) * F, :] = jnp.dot(
                fk[h * F : (h + 1) * F, :], src[:, h * DV : (h + 1) * DV], preferred_element_type=F32
            )

    sent = []
    wa = []
    wb = {1: [], 2: [], 3: []}

    def onward(shard):
        n = 6 * (shard - 1)
        for d in range(1, 4):
            src = wf.at[shard, zc, :, core, :, 0:256]
            cp = remote(src, src, wb_s.at[n], wb_r.at[n], zpeer(d))
            cp.start()
            wb[shard].append(cp)
            src = wf.at[shard, :, yc, core, :, 256:512]
            cp = remote(src, src, wb_s.at[n + 1], wb_r.at[n + 1], ypeer(d))
            cp.start()
            wb[shard].append(cp)
            n += 2

    def across_cores(shard):
        for cp in wb[shard]:
            cp.wait()
        src = wf.at[shard, :, :, core]
        cp = remote(src, src, wc_s.at[shard - 1], wc_r.at[shard - 1], (sib, t))
        cp.start()
        return cp

    ekcopy.wait()
    for i, (d, half) in enumerate(tiles):
        c = near(d) * 2 + half
        if i == 3:
            halo.wait()
            tl[0:8, :] = jnp.where(s == 0, 0.0, tl[0:8, :])
        if i == 2:
            for cp in wx:
                cp.wait()
            for n in range(1, 4):
                src = wf.at[1:4, zc, yc, core, :, 0:256]
                cp = remote(src, src, wa_s.at[n - 1], wa_r.at[n - 1], ypeer(n))
                cp.start()
                wa.append(cp)
                src = wf.at[1:4, zc, yc, core, :, 256:512]
                cp = remote(src, src, wa_s.at[n + 2], wa_r.at[n + 2], zpeer(n))
                cp.start()
                wa.append(cp)
        if i == 5:
            for cp in wa:
                cp.wait()
            onward(1)
        xcopies[i].wait()
        tile = mx.at[i] if d else ga.at[t, half]
        mix(i, c, tile)
        if d:
            cp = remote(tile, ga.at[t, half], a_s.at[half, d - 1], a_r.at[half, d - 1], xpeer(d))
            cp.start()
            sent.append(cp)
        states(c, tile)

    run = jnp.zeros((HL * F, DV), F32)
    for c in range(NC):
        part = sc[c]
        if c % 2 == 0:
            sc[c] = run
        run = run + part
    for k in range(CHIPS):
        sb[k] = run[k * ROWS : (k + 1) * ROWS, :].astype(BF16)

    def spread(i, carry):
        k = lax.rem(chip + i, CHIPS)
        remote(sb.at[k], r1.at[s], s1_s, s1_r, (2 * k, t)).start()
        return carry

    lax.fori_loop(1, CHIPS, spread, 0)

    @pl.when(core == 1)
    def _():
        remote(sb.at[chip], r1.at[s], s3_s, s1_r, (s - 1, t)).start()

    @pl.when(core == 0)
    def _():
        r1[s] = sb[chip]

    eqcopy.wait()
    pos = lax.broadcasted_iota(jnp.int32, (C, C), 0) >= lax.broadcasted_iota(jnp.int32, (C, C), 1)

    def arrived(d, half):
        n = TP - d - 1
        remote(mx.at[0], ga.at[near(d), half], a_s.at[half, n], a_r.at[half, n], xpeer(d)).wait_recv()

    def scores(q, kt, h):
        parts = []
        if h > 0:
            parts.append(jnp.zeros((32 * h, C), BF16))
        parts.append(kt[32 * h + 16 : 32 * h + 32, :])
        parts.append(jnp.zeros((QW - 32 * h - 16, C), BF16))
        up = jnp.dot(q, jnp.concatenate(parts, axis=0), preferred_element_type=F32) + 1.0
        return up * up * 0.5 + 0.5

    def keys(src):
        return (jnp.transpose(src[:, VW:].astype(F32)) * 0.25).astype(BF16)

    def local(d, half):
        src = ga.at[near(d), half]
        q = src[:, VW:]
        qe = jnp.concatenate([q, jnp.ones((C, FP - QW), BF16)], axis=1)
        kt = keys(src)
        for h in range(HL):
            fq[half, d, :, h * FP : (h + 1) * FP] = (
                jnp.dot(qe, eqv[0, :, h * FP : (h + 1) * FP], preferred_element_type=F32)
                * jnp.dot(qe, eqv[1, :, h * FP : (h + 1) * FP], preferred_element_type=F32)
            ).astype(BF16)
            w = jnp.where(pos, scores(q, kt, h), 0.0).astype(BF16)
            nl[half, d, :, h * DV : (h + 1) * DV] = jnp.dot(
                w, src[:, h * DV : (h + 1) * DV], preferred_element_type=F32
            )

    def across(d):
        q = ga[near(d), 1, :, VW:]
        src = ga.at[near(d), 0]
        kt = keys(src)
        for h in range(HL):
            w = scores(q, kt, h).astype(BF16)
            nl[1, d, :, h * DV : (h + 1) * DV] += jnp.dot(
                w, src[:, h * DV : (h + 1) * DV], preferred_element_type=F32
            )

    local(0, 1)
    local(0, 0)
    across(0)

    @pl.when(core == 0)
    def _():
        pltpu.make_async_copy(r1.at[0 : SEQ - 1], r1.at[0 : SEQ - 1], s1_r).wait()
        acc = jnp.zeros((ROWS, DV), F32)
        for k in range(SEQ):
            p2[k // 2, k % 2] = acc.astype(BF16)
            acc = acc + r1[k].astype(F32)
        r2[chip] = p2[chip]

        def back(i, carry):
            k = lax.rem(chip + i, CHIPS)
            remote(p2.at[k], r2.at[chip], s2_s, s2_r, (2 * k, t)).start()
            return carry

        lax.fori_loop(1, CHIPS, back, 0)

    pltpu.make_async_copy(sb.at[0 : CHIPS - 1], sb.at[0 : CHIPS - 1], s1_s).wait()
    for d in (3, 1, 2):
        arrived(d, 1)
        local(d, 1)

    fwd = remote(r2, r2, s3_s, s3_r, (sib, t))

    @pl.when(core == 0)
    def _():
        pltpu.make_async_copy(p2.at[0 : CHIPS - 1], p2.at[0 : CHIPS - 1], s2_s).wait()
        pltpu.make_async_copy(r2.at[0 : CHIPS - 1], r2.at[0 : CHIPS - 1], s2_r).wait()
        fwd.start()

    @pl.when(core == 1)
    def _():
        remote(sb.at[chip], r1.at[s], s3_s, s1_r, (s - 1, t)).wait_send()
        fwd.wait_recv()

    onward(3)

    pcopies = {}
    for d in (1, 3, 2, 0):
        n = near(d)
        for k in range(CHIPS):
            h, o = k // 4, (k % 4) * ROWS
            val = (r2[k, core].astype(F32) + sc[2 * n, k * ROWS : (k + 1) * ROWS, :]).astype(BF16)
            if d:
                ps[d - 1, h, o : o + ROWS, :] = val
            else:
                pp[t, h, o : o + ROWS, :] = val
        if d:
            cp = remote(ps.at[d - 1], pp.at[t, :, 0:F, :], q_s.at[d - 1], q_r.at[d - 1], xpeer(d))
            cp.start()
            pcopies[d] = cp
    wc = {1: across_cores(1)}
    onward(2)

    for d in (3, 1, 2):
        arrived(d, 0)
        local(d, 0)
        across(d)

    @pl.when(core == 0)
    def _():
        fwd.wait_send()


    results = []
    own = []
    for half in range(2):
        for d in (0, 3, 1, 2):
            if half == 0 and d:
                pcopies[TP - d].wait_recv()
            for h in range(HL):
                num = nl[half, d, :, h * DV : (h + 1) * DV] + jnp.dot(
                    fq[half, d, :, h * FP : (h + 1) * FP], pp[near(d), h], preferred_element_type=F32
                )
                spread_ = jnp.mean(num * num, axis=-1, keepdims=True)
                gh[half, d, :, h * DV : (h + 1) * DV] = (num * lax.rsqrt(spread_ + EPS)).astype(BF16)
        for n, d in enumerate((1, 3, 2, 0)):
            if half == 0:
                if d:
                    wc[d].wait()
                else:
                    wocopy.wait()
            if half == 0 and n == 0:
                wc[3] = across_cores(3)
            if half == 0 and n == 1:
                wc[2] = across_cores(2)
            acc = jnp.zeros((C, 512), F32)
            for p in range(TP):
                acc = acc + jnp.dot(
                    gh[half, p], wf[d, near(p)].reshape(512, 512), preferred_element_type=F32
                )
            ob[half, n] = acc.astype(BF16)
            rows = out_ref.at[pl.ds(pl.multiple_of(t * 512 + half * C, C), C)]
            if d:
                cp = remote(ob.at[half, n], rows, b_s.at[half, d - 1], b_r.at[half, d - 1], xpeer(d))
                cp.start()
                results.append(cp)
            else:
                cp = pltpu.make_async_copy(ob.at[half, n], rows, own_s.at[half])
                cp.start()
                own.append(cp)

    for cp in sent + results + list(pcopies.values()):
        cp.wait_send()
    for half in range(2):
        for d in range(1, TP):
            rows = out_ref.at[pl.ds(pl.multiple_of(near(TP - d) * 512 + half * C, C), C)]
            remote(ob.at[half, 0], rows, b_s.at[half, 0], b_r.at[half, d - 1], xpeer(d)).wait_recv()
    for cp in own:
        cp.wait()


def copy_kernel(src_ref, dst_ref, sem):
    copies = []
    for i in range(8):
        rows = pl.ds(i * (T // 8), T // 8)
        cp = pltpu.make_async_copy(src_ref.at[rows], dst_ref.at[rows], sem.at[i])
        cp.start()
        copies.append(cp)
    for cp in copies:
        cp.wait()


def body(tokens, gain, w_in, conv_taps, w_out):
    wt = jnp.transpose(w_in, (1, 2, 0)).reshape(HL * 160, D)
    eq, ek = feature_maps()
    hbm = pl.BlockSpec(memory_space=pl.ANY)
    vmem = pl.BlockSpec(memory_space=pltpu.VMEM)
    dma = pltpu.SemaphoreType.DMA
    width = VW + QW
    result = pl.pallas_call(
        kernel,
        out_shape=jax.ShapeDtypeStruct((T, 512), BF16),
        in_specs=[hbm, vmem, hbm, vmem, hbm, hbm, hbm],
        out_specs=hbm,
        scratch_shapes=[
            pltpu.VMEM((NC, C, D), BF16),
            pltpu.VMEM((8 * NC, D), BF16),
            pltpu.VMEM((width, D), BF16),
            pltpu.VMEM((width, D), BF16),
            pltpu.VMEM((2, FP, HL * FP), BF16),
            pltpu.VMEM((2, HL * F, FP), BF16),
            pltpu.VMEM((8, width), F32),
            pltpu.VMEM((2, 8 + C, width), F32),
            pltpu.VMEM((8 + 8 * NC, width), F32),
            pltpu.VMEM((6, C, width), BF16),
            pltpu.VMEM((TP, 2, C, width), BF16),
            pltpu.VMEM((NC, HL * F, DV), F32),
            pltpu.VMEM((2, TP, C, VW), F32),
            pltpu.VMEM((2, TP, C, HL * FP), BF16),
            pltpu.VMEM((CHIPS, ROWS, DV), BF16),
            pltpu.VMEM((SEQ, ROWS, DV), BF16),
            pltpu.VMEM((CHIPS, 2, ROWS, DV), BF16),
            pltpu.VMEM((CHIPS, 2, ROWS, DV), BF16),
            pltpu.VMEM((3, HL, F, DV), BF16),
            pltpu.VMEM((TP, HL, FP, DV), BF16),
            pltpu.VMEM((4, 4, 4, 2, 64, 512), BF16),
            pltpu.VMEM((2, TP, C, VW), BF16),
            pltpu.VMEM((2, 4, C, 512), BF16),
            dma((3 + NC,)), dma((HL,)), dma((NC,)), dma, dma, dma, dma, dma, dma, dma, dma, dma,
            dma((3,)), dma((3,)), dma((6,)), dma((6,)), dma((18,)), dma((18,)), dma((3,)), dma((3,)),
            dma((2, 3)), dma((2, 3)), dma((3,)), dma((3,)), dma((2, 3)), dma((2, 3)), dma((2,)),
        ],
        compiler_params=pltpu.CompilerParams(
            collective_id=0, has_side_effects=True, vmem_limit_bytes=59 * 1024 * 1024
        ),
    )(
        tokens, gain, wt, conv_taps, w_out.reshape(4, 4, 2, 64, 512),
        jnp.asarray(eq), jnp.asarray(ek),
    )
    return pl.pallas_call(
        copy_kernel,
        out_shape=jax.ShapeDtypeStruct((T, 512), BF16),
        in_specs=[hbm],
        out_specs=hbm,
        scratch_shapes=[dma((8,))],
    )(result)


def solution(mesh):
    return jax.shard_map(
        body,
        mesh=mesh,
        in_specs=(P("seq", None), P(), P(None, "tp", None), P(None, "tp", None), P(None, "tp")),
        out_specs=P("seq", "tp"),
        check_vma=False,
    )
```

```python
import functools
import math

import jax
import jax.numpy as jnp
import numpy as np
from jax import lax
from jax.experimental import pallas as pl
from jax.experimental.pallas import tpu as pltpu
from jax.sharding import PartitionSpec as P

DK = 16
DV = 128
HL = 4
T = 2048
D = 2048
C = 256
NC = T // C
F = 160
FP = 256
VW = HL * DV
QW = HL * 2 * DK
SEQ = 32
TP = 4
CHIPS = SEQ // 2
ROWS = HL * F // CHIPS
EPS = 1e-06
MESH = pl.DeviceIdType.MESH
F32 = jnp.float32
BF16 = jnp.bfloat16


def feature_maps():
    eq = np.zeros((2, FP, HL * FP), np.float32)
    ek = np.zeros((2, HL * F, FP), np.float32)
    one = QW
    for h in range(HL):
        q0, k0 = 2 * DK * h, 2 * DK * h + DK
        f = 0
        for i in range(DK):
            for j in range(i, DK):
                eq[0, q0 + i, h * FP + f] = (1.0 if i == j else 2.0) / 32.0
                eq[1, q0 + j, h * FP + f] = 1.0
                ek[0, h * F + f, k0 + i] = 1.0
                ek[1, h * F + f, k0 + j] = 1.0
                f += 1
        for i in range(DK):
            eq[0, q0 + i, h * FP + f] = 0.25
            eq[1, one, h * FP + f] = 1.0
            ek[0, h * F + f, k0 + i] = 1.0
            ek[1, h * F + f, one] = 1.0
            f += 1
        eq[0, one, h * FP + f] = 1.0
        eq[1, one, h * FP + f] = 1.0
        ek[0, h * F + f, one] = 1.0
        ek[1, h * F + f, one] = 1.0
    return eq.astype(jnp.bfloat16), ek.astype(jnp.bfloat16)


def kernel(
    x_hbm, gain_ref, wt_hbm, taps_ref, wo_hbm, eq_hbm, ek_hbm,
    out_ref,
    xv, xt8, wv, wg, eqv, ekv, taps, pf, tl, mx, ga, sc, nl, fq, sb, r1, p2, r2, ps, pp, wf, gh, ob,
    in_sem, x_sem, wo_sem, halo_s, halo_r, s1_s, s1_r, s2_s, s2_r, s3_s, s3_r,
    wx_s, wx_r, wa_s, wa_r, wb_s, wb_r, wc_s, wc_r, a_s, a_r, q_s, q_r, b_s, b_r, own_s,
):
    s = lax.axis_index("seq")
    t = lax.axis_index("tp")
    chip = s // 2
    core = s % 2
    zc = s // 8
    yc = (s // 2) % 4
    sib = s + 1 - 2 * core

    def remote(src, dst, ss, rs, dev):
        return pltpu.make_async_remote_copy(
            src_ref=src, dst_ref=dst, send_sem=ss, recv_sem=rs, device_id=dev, device_id_type=MESH
        )

    def near(d):
        return lax.rem(t + d, TP)

    def xpeer(d):
        return (s, near(d))

    def ypeer(d):
        return (zc * 8 + lax.rem(yc + d, 4) * 2 + core, t)

    def zpeer(d):
        return (lax.rem(zc + d, 4) * 8 + yc * 2 + core, t)

    tiles = [(d, half) for half in (1, 0) for d in (1, 3, 2)] + [(0, 1), (0, 0)]

    wcopy = pltpu.make_async_copy(wt_hbm, wv, in_sem.at[0])
    wcopy.start()
    tcopies = []
    for c in range(NC):
        cp = pltpu.make_async_copy(x_hbm.at[pl.ds(c * C + C - 8, 8)], xt8.at[pl.ds(8 * c, 8)], in_sem.at[3 + c])
        cp.start()
        tcopies.append(cp)
    xcopies = []
    for i, (d, half) in enumerate(tiles):
        base = pl.multiple_of((near(d) * 2 + half) * C, C)
        cp = pltpu.make_async_copy(x_hbm.at[pl.ds(base, C)], xv.at[i], x_sem.at[i])
        cp.start()
        xcopies.append(cp)
    ekcopy = pltpu.make_async_copy(ek_hbm, ekv, in_sem.at[1])
    ekcopy.start()
    eqcopy = pltpu.make_async_copy(eq_hbm, eqv, in_sem.at[2])
    eqcopy.start()
    wocopy = pltpu.make_async_copy(wo_hbm, wf.at[0], wo_sem)
    wocopy.start()

    barrier = pltpu.get_barrier_semaphore()

    def greet(j, carry):
        pl.semaphore_signal(barrier, inc=1, device_id=(lax.rem(s + j, SEQ), t), device_id_type=MESH)
        return carry

    lax.fori_loop(1, SEQ, greet, 0)
    for d in range(1, TP):
        pl.semaphore_signal(barrier, inc=1, device_id=xpeer(d), device_id_type=MESH)

    pp[:, :, F:, :] = jnp.zeros((TP, HL, FP - F, DV), BF16)

    row = lax.broadcasted_iota(jnp.int32, (160, 128), 0)
    col = lax.broadcasted_iota(jnp.int32, (160, 128), 1)
    pick_v = (row == col + 2 * DK).astype(F32).astype(BF16)
    for k in range(3):
        tk = taps_ref[k]
        tv = jnp.dot(tk, pick_v, preferred_element_type=F32)
        tq = jnp.zeros((1, QW), F32)
        for h in range(HL):
            taps[k : k + 1, h * DV : (h + 1) * DV] = tv[h : h + 1, :]
            pick_q = ((row + 2 * DK * h == col) & (row < 2 * DK)).astype(F32).astype(BF16)
            tq = tq + jnp.dot(tk, pick_q, preferred_element_type=F32)[h : h + 1, :]
        taps[k : k + 1, VW:] = tq

    wcopy.wait()
    gain = gain_ref[...].astype(F32)[None, :]
    for h in range(HL):
        for r in range(0, 160, 32):
            dst = VW + 32 * h if r == 0 else h * DV + r - 32
            src = h * 160 + r
            wg[dst : dst + 32, :] = (wv[src : src + 32, :].astype(F32) * gain).astype(BF16)

    def project(xt):
        xf = xt.astype(F32)
        scale = lax.rsqrt(jnp.mean(xf * xf, axis=-1, keepdims=True) + EPS)
        pr = lax.dot_general(xt, wg[...], (((1,), (1,)), ((), ())), preferred_element_type=F32)
        return (pr * scale).astype(BF16).astype(F32)

    for cp in tcopies:
        cp.wait()
    tl[8:, :] = project(xt8[...])

    pl.semaphore_wait(barrier, SEQ - 1 + TP - 1)
    halo = remote(tl.at[pl.ds(8 * NC, 8)], tl.at[pl.ds(0, 8)], halo_s, halo_r, (lax.rem(s + 1, SEQ), t))
    halo.start()
    wx = []
    for d in range(1, TP):
        cp = remote(
            wo_hbm.at[zc, yc, core], wf.at[TP - d, zc, yc, core], wx_s.at[d - 1], wx_r.at[d - 1], xpeer(d)
        )
        cp.start()
        wx.append(cp)

    def mix(i, c, dst):
        buf = pf.at[i % 2]
        buf[0:8, :] = tl[pl.ds(pl.multiple_of(c * 8, 8), 8), :]
        buf[8:, :] = project(xv[i])
        mixed = (
            buf[6 : 6 + C, :] * taps[0:1, :] + buf[7 : 7 + C, :] * taps[1:2, :] + buf[8 : 8 + C, :] * taps[2:3, :]
        )
        dst[...] = mixed.astype(BF16)

    def states(c, src):
        qe = jnp.concatenate(
            [jnp.transpose(src[:, VW:].astype(F32)).astype(BF16), jnp.ones((FP - QW, C), BF16)], axis=0
        )
        fk = (
            jnp.dot(ekv[0], qe, preferred_element_type=F32) * jnp.dot(ekv[1], qe, preferred_element_type=F32)
        ).astype(BF16)
        for h in range(HL):
            sc[c, h * F : (h + 1) * F, :] = jnp.dot(
                fk[h * F : (h + 1) * F, :], src[:, h * DV : (h + 1) * DV], preferred_element_type=F32
            )

    sent = []
    wa = []
    wb = {1: [], 2: [], 3: []}

    def onward(shard):
        n = 6 * (shard - 1)
        for d in range(1, 4):
            src = wf.at[shard, zc, :, core, :, 0:256]
            cp = remote(src, src, wb_s.at[n], wb_r.at[n], zpeer(d))
            cp.start()
            wb[shard].append(cp)
            src = wf.at[shard, :, yc, core, :, 256:512]
            cp = remote(src, src, wb_s.at[n + 1], wb_r.at[n + 1], ypeer(d))
            cp.start()
            wb[shard].append(cp)
            n += 2

    def across_cores(shard):
        for cp in wb[shard]:
            cp.wait()
        src = wf.at[shard, :, :, core]
        cp = remote(src, src, wc_s.at[shard - 1], wc_r.at[shard - 1], (sib, t))
        cp.start()
        return cp

    ekcopy.wait()
    for i, (d, half) in enumerate(tiles):
        c = near(d) * 2 + half
        if i == 3:
            halo.wait()
            tl[0:8, :] = jnp.where(s == 0, 0.0, tl[0:8, :])
        if i == 2:
            for cp in wx:
                cp.wait()
            for n in range(1, 4):
                src = wf.at[1:4, zc, yc, core, :, 0:256]
                cp = remote(src, src, wa_s.at[n - 1], wa_r.at[n - 1], ypeer(n))
                cp.start()
                wa.append(cp)
                src = wf.at[1:4, zc, yc, core, :, 256:512]
                cp = remote(src, src, wa_s.at[n + 2], wa_r.at[n + 2], zpeer(n))
                cp.start()
                wa.append(cp)
        if i == 5:
            for cp in wa:
                cp.wait()
            onward(1)
        xcopies[i].wait()
        tile = mx.at[i] if d else ga.at[t, half]
        mix(i, c, tile)
        if d:
            cp = remote(tile, ga.at[t, half], a_s.at[half, d - 1], a_r.at[half, d - 1], xpeer(d))
            cp.start()
            sent.append(cp)
        states(c, tile)

    run = jnp.zeros((HL * F, DV), F32)
    for c in range(NC):
        part = sc[c]
        if c % 2 == 0:
            sc[c] = run
        run = run + part
    for k in range(CHIPS):
        sb[k] = run[k * ROWS : (k + 1) * ROWS, :].astype(BF16)

    def spread(i, carry):
        k = lax.rem(chip + i, CHIPS)
        remote(sb.at[k], r1.at[s], s1_s, s1_r, (2 * k, t)).start()
        return carry

    lax.fori_loop(1, CHIPS, spread, 0)

    @pl.when(core == 1)
    def _():
        remote(sb.at[chip], r1.at[s], s3_s, s1_r, (s - 1, t)).start()

    @pl.when(core == 0)
    def _():
        r1[s] = sb[chip]

    eqcopy.wait()
    pos = lax.broadcasted_iota(jnp.int32, (C, C), 0) >= lax.broadcasted_iota(jnp.int32, (C, C), 1)

    def arrived(d, half):
        n = TP - d - 1
        remote(mx.at[0], ga.at[near(d), half], a_s.at[half, n], a_r.at[half, n], xpeer(d)).wait_recv()

    def scores(q, kt, h):
        parts = []
        if h > 0:
            parts.append(jnp.zeros((32 * h, C), BF16))
        parts.append(kt[32 * h + 16 : 32 * h + 32, :])
        parts.append(jnp.zeros((QW - 32 * h - 16, C), BF16))
        up = jnp.dot(q, jnp.concatenate(parts, axis=0), preferred_element_type=F32) + 1.0
        return up * up * 0.5 + 0.5

    def keys(src):
        return (jnp.transpose(src[:, VW:].astype(F32)) * 0.25).astype(BF16)

    def local(d, half):
        src = ga.at[near(d), half]
        q = src[:, VW:]
        qe = jnp.concatenate([q, jnp.ones((C, FP - QW), BF16)], axis=1)
        kt = keys(src)
        for h in range(HL):
            fq[half, d, :, h * FP : (h + 1) * FP] = (
                jnp.dot(qe, eqv[0, :, h * FP : (h + 1) * FP], preferred_element_type=F32)
                * jnp.dot(qe, eqv[1, :, h * FP : (h + 1) * FP], preferred_element_type=F32)
            ).astype(BF16)
            w = jnp.where(pos, scores(q, kt, h), 0.0).astype(BF16)
            nl[half, d, :, h * DV : (h + 1) * DV] = jnp.dot(
                w, src[:, h * DV : (h + 1) * DV], preferred_element_type=F32
            )

    def across(d):
        q = ga[near(d), 1, :, VW:]
        src = ga.at[near(d), 0]
        kt = keys(src)
        for h in range(HL):
            w = scores(q, kt, h).astype(BF16)
            nl[1, d, :, h * DV : (h + 1) * DV] += jnp.dot(
                w, src[:, h * DV : (h + 1) * DV], preferred_element_type=F32
            )

    local(0, 1)
    local(0, 0)
    across(0)

    @pl.when(core == 0)
    def _():
        pltpu.make_async_copy(r1.at[0 : SEQ - 1], r1.at[0 : SEQ - 1], s1_r).wait()
        acc = jnp.zeros((ROWS, DV), F32)
        for k in range(SEQ):
            p2[k // 2, k % 2] = acc.astype(BF16)
            acc = acc + r1[k].astype(F32)
        r2[chip] = p2[chip]

        def back(i, carry):
            k = lax.rem(chip + i, CHIPS)
            remote(p2.at[k], r2.at[chip], s2_s, s2_r, (2 * k, t)).start()
            return carry

        lax.fori_loop(1, CHIPS, back, 0)

    pltpu.make_async_copy(sb.at[0 : CHIPS - 1], sb.at[0 : CHIPS - 1], s1_s).wait()
    for d in (3, 1, 2):
        arrived(d, 1)
        local(d, 1)

    fwd = remote(r2, r2, s3_s, s3_r, (sib, t))

    @pl.when(core == 0)
    def _():
        pltpu.make_async_copy(p2.at[0 : CHIPS - 1], p2.at[0 : CHIPS - 1], s2_s).wait()
        pltpu.make_async_copy(r2.at[0 : CHIPS - 1], r2.at[0 : CHIPS - 1], s2_r).wait()
        fwd.start()

    @pl.when(core == 1)
    def _():
        remote(sb.at[chip], r1.at[s], s3_s, s1_r, (s - 1, t)).wait_send()
        fwd.wait_recv()

    pcopies = []
    for d in (1, 3, 2, 0):
        n = near(d)
        for k in range(CHIPS):
            h, o = k // 4, (k % 4) * ROWS
            val = (r2[k, core].astype(F32) + sc[2 * n, k * ROWS : (k + 1) * ROWS, :]).astype(BF16)
            if d:
                ps[d - 1, h, o : o + ROWS, :] = val
            else:
                pp[t, h, o : o + ROWS, :] = val
        if d:
            cp = remote(ps.at[d - 1], pp.at[t, :, 0:F, :], q_s.at[d - 1], q_r.at[d - 1], xpeer(d))
            cp.start()
            pcopies.append(cp)
    wc = {1: across_cores(1)}
    onward(3)
    onward(2)

    for d in (3, 1, 2):
        arrived(d, 0)
        local(d, 0)
        across(d)

    @pl.when(core == 0)
    def _():
        fwd.wait_send()

    for cp in pcopies:
        cp.wait()

    results = []
    own = []
    for half in range(2):
        for d in range(TP):
            for h in range(HL):
                num = nl[half, d, :, h * DV : (h + 1) * DV] + jnp.dot(
                    fq[half, d, :, h * FP : (h + 1) * FP], pp[near(d), h], preferred_element_type=F32
                )
                spread_ = jnp.mean(num * num, axis=-1, keepdims=True)
                gh[half, d, :, h * DV : (h + 1) * DV] = (num * lax.rsqrt(spread_ + EPS)).astype(BF16)
        for n, d in enumerate((1, 3, 2, 0)):
            if half == 0:
                if d:
                    wc[d].wait()
                else:
                    wocopy.wait()
            if half == 0 and n == 0:
                wc[3] = across_cores(3)
            if half == 0 and n == 1:
                wc[2] = across_cores(2)
            acc = jnp.zeros((C, 512), F32)
            for p in range(TP):
                acc = acc + jnp.dot(
                    gh[half, p], wf[d, near(p)].reshape(512, 512), preferred_element_type=F32
                )
            ob[half, n] = acc.astype(BF16)
            rows = out_ref.at[pl.ds(pl.multiple_of(t * 512 + half * C, C), C)]
            if d:
                cp = remote(ob.at[half, n], rows, b_s.at[half, d - 1], b_r.at[half, d - 1], xpeer(d))
                cp.start()
                results.append(cp)
            else:
                cp = pltpu.make_async_copy(ob.at[half, n], rows, own_s.at[half])
                cp.start()
                own.append(cp)

    for cp in sent + results:
        cp.wait_send()
    for half in range(2):
        for d in range(1, TP):
            rows = out_ref.at[pl.ds(pl.multiple_of(near(TP - d) * 512 + half * C, C), C)]
            remote(ob.at[half, 0], rows, b_s.at[half, 0], b_r.at[half, d - 1], xpeer(d)).wait_recv()
    for cp in own:
        cp.wait()


def copy_kernel(src_ref, dst_ref, buf, in_sem, out_sem):
    loads, stores = [], []
    for i in range(8):
        rows = pl.ds(i * (T // 8), T // 8)
        loads.append(pltpu.make_async_copy(src_ref.at[rows], buf.at[rows], in_sem.at[i]))
        stores.append(pltpu.make_async_copy(buf.at[rows], dst_ref.at[rows], out_sem.at[i]))
    for cp in loads:
        cp.start()
    for load, store in zip(loads, stores):
        load.wait()
        store.start()
    for cp in stores:
        cp.wait()


def body(tokens, gain, w_in, conv_taps, w_out):
    wt = jnp.transpose(w_in, (1, 2, 0)).reshape(HL * 160, D)
    eq, ek = feature_maps()
    hbm = pl.BlockSpec(memory_space=pl.ANY)
    vmem = pl.BlockSpec(memory_space=pltpu.VMEM)
    dma = pltpu.SemaphoreType.DMA
    width = VW + QW
    result = pl.pallas_call(
        kernel,
        out_shape=jax.ShapeDtypeStruct((T, 512), BF16),
        in_specs=[hbm, vmem, hbm, vmem, hbm, hbm, hbm],
        out_specs=hbm,
        scratch_shapes=[
            pltpu.VMEM((NC, C, D), BF16),
            pltpu.VMEM((8 * NC, D), BF16),
            pltpu.VMEM((width, D), BF16),
            pltpu.VMEM((width, D), BF16),
            pltpu.VMEM((2, FP, HL * FP), BF16),
            pltpu.VMEM((2, HL * F, FP), BF16),
            pltpu.VMEM((8, width), F32),
            pltpu.VMEM((2, 8 + C, width), F32),
            pltpu.VMEM((8 + 8 * NC, width), F32),
            pltpu.VMEM((6, C, width), BF16),
            pltpu.VMEM((TP, 2, C, width), BF16),
            pltpu.VMEM((NC, HL * F, DV), F32),
            pltpu.VMEM((2, TP, C, VW), F32),
            pltpu.VMEM((2, TP, C, HL * FP), BF16),
            pltpu.VMEM((CHIPS, ROWS, DV), BF16),
            pltpu.VMEM((SEQ, ROWS, DV), BF16),
            pltpu.VMEM((CHIPS, 2, ROWS, DV), BF16),
            pltpu.VMEM((CHIPS, 2, ROWS, DV), BF16),
            pltpu.VMEM((3, HL, F, DV), BF16),
            pltpu.VMEM((TP, HL, FP, DV), BF16),
            pltpu.VMEM((4, 4, 4, 2, 64, 512), BF16),
            pltpu.VMEM((2, TP, C, VW), BF16),
            pltpu.VMEM((2, 4, C, 512), BF16),
            dma((3 + NC,)), dma((NC,)), dma, dma, dma, dma, dma, dma, dma, dma, dma,
            dma((3,)), dma((3,)), dma((6,)), dma((6,)), dma((18,)), dma((18,)), dma((3,)), dma((3,)),
            dma((2, 3)), dma((2, 3)), dma((3,)), dma((3,)), dma((2, 3)), dma((2, 3)), dma((2,)),
        ],
        compiler_params=pltpu.CompilerParams(
            collective_id=0, has_side_effects=True, vmem_limit_bytes=59 * 1024 * 1024
        ),
    )(
        tokens, gain, wt, conv_taps, w_out.reshape(4, 4, 2, 64, 512),
        jnp.asarray(eq), jnp.asarray(ek),
    )
    return pl.pallas_call(
        copy_kernel,
        out_shape=jax.ShapeDtypeStruct((T, 512), BF16),
        in_specs=[hbm],
        out_specs=hbm,
        scratch_shapes=[pltpu.VMEM((T, 512), BF16), dma((8,)), dma((8,))],
    )(result)


def solution(mesh):
    return jax.shard_map(
        body,
        mesh=mesh,
        in_specs=(P("seq", None), P(), P(None, "tp", None), P(None, "tp", None), P(None, "tp")),
        out_specs=P("seq", "tp"),
        check_vma=False,
    )
```

```python
import functools
import math

import jax
import jax.numpy as jnp
import numpy as np
from jax import lax
from jax.experimental import pallas as pl
from jax.experimental.pallas import tpu as pltpu
from jax.sharding import PartitionSpec as P

DK = 16
DV = 128
HL = 4
T = 2048
D = 2048
C = 256
NC = T // C
F = 160
FP = 256
VW = HL * DV
QW = HL * 2 * DK
SEQ = 32
TP = 4
CHIPS = SEQ // 2
ROWS = HL * F // CHIPS
EPS = 1e-06
MESH = pl.DeviceIdType.MESH
F32 = jnp.float32
BF16 = jnp.bfloat16


def feature_maps():
    eq = np.zeros((2, FP, HL * FP), np.float32)
    ek = np.zeros((2, HL * F, FP), np.float32)
    one = QW
    for h in range(HL):
        q0, k0 = 2 * DK * h, 2 * DK * h + DK
        f = 0
        for i in range(DK):
            for j in range(i, DK):
                eq[0, q0 + i, h * FP + f] = (1.0 if i == j else 2.0) / 32.0
                eq[1, q0 + j, h * FP + f] = 1.0
                ek[0, h * F + f, k0 + i] = 1.0
                ek[1, h * F + f, k0 + j] = 1.0
                f += 1
        for i in range(DK):
            eq[0, q0 + i, h * FP + f] = 0.25
            eq[1, one, h * FP + f] = 1.0
            ek[0, h * F + f, k0 + i] = 1.0
            ek[1, h * F + f, one] = 1.0
            f += 1
        eq[0, one, h * FP + f] = 1.0
        eq[1, one, h * FP + f] = 1.0
        ek[0, h * F + f, one] = 1.0
        ek[1, h * F + f, one] = 1.0
    return eq.astype(jnp.bfloat16), ek.astype(jnp.bfloat16)


def kernel(
    x_hbm, gain_ref, wt_hbm, taps_ref, wo_hbm, eq_hbm, ek_hbm,
    out_ref,
    xv, xt8, wv, wg, eqv, ekv, taps, pf, tl, mx, ga, sc, nl, fq, sb, r1, p2, r2, ps, pp, wf, gh, ob,
    in_sem, x_sem, wo_sem, halo_s, halo_r, s1_s, s1_r, s2_s, s2_r, s3_s, s3_r,
    wx_s, wx_r, wa_s, wa_r, wb_s, wb_r, wc_s, wc_r, a_s, a_r, q_s, q_r, b_s, b_r, own_s,
):
    s = lax.axis_index("seq")
    t = lax.axis_index("tp")
    chip = s // 2
    core = s % 2
    zc = s // 8
    yc = (s // 2) % 4
    sib = s + 1 - 2 * core

    def remote(src, dst, ss, rs, dev):
        return pltpu.make_async_remote_copy(
            src_ref=src, dst_ref=dst, send_sem=ss, recv_sem=rs, device_id=dev, device_id_type=MESH
        )

    def near(d):
        return lax.rem(t + d, TP)

    def xpeer(d):
        return (s, near(d))

    def ypeer(d):
        return (zc * 8 + lax.rem(yc + d, 4) * 2 + core, t)

    def zpeer(d):
        return (lax.rem(zc + d, 4) * 8 + yc * 2 + core, t)

    tiles = [(d, half) for half in (1, 0) for d in (1, 3, 2)] + [(0, 1), (0, 0)]

    wcopy = pltpu.make_async_copy(wt_hbm, wv, in_sem.at[0])
    wcopy.start()
    tcopies = []
    for c in range(NC):
        cp = pltpu.make_async_copy(x_hbm.at[pl.ds(c * C + C - 8, 8)], xt8.at[pl.ds(8 * c, 8)], in_sem.at[3 + c])
        cp.start()
        tcopies.append(cp)
    xcopies = []
    for i, (d, half) in enumerate(tiles):
        base = pl.multiple_of((near(d) * 2 + half) * C, C)
        cp = pltpu.make_async_copy(x_hbm.at[pl.ds(base, C)], xv.at[i], x_sem.at[i])
        cp.start()
        xcopies.append(cp)
    ekcopy = pltpu.make_async_copy(ek_hbm, ekv, in_sem.at[1])
    ekcopy.start()
    eqcopy = pltpu.make_async_copy(eq_hbm, eqv, in_sem.at[2])
    eqcopy.start()
    wocopy = pltpu.make_async_copy(wo_hbm, wf.at[0], wo_sem)
    wocopy.start()

    barrier = pltpu.get_barrier_semaphore()

    def greet(j, carry):
        pl.semaphore_signal(barrier, inc=1, device_id=(lax.rem(s + j, SEQ), t), device_id_type=MESH)
        return carry

    lax.fori_loop(1, SEQ, greet, 0)
    for d in range(1, TP):
        pl.semaphore_signal(barrier, inc=1, device_id=xpeer(d), device_id_type=MESH)

    pp[:, :, F:, :] = jnp.zeros((TP, HL, FP - F, DV), BF16)

    row = lax.broadcasted_iota(jnp.int32, (160, 128), 0)
    col = lax.broadcasted_iota(jnp.int32, (160, 128), 1)
    pick_v = (row == col + 2 * DK).astype(F32).astype(BF16)
    for k in range(3):
        tk = taps_ref[k]
        tv = jnp.dot(tk, pick_v, preferred_element_type=F32)
        tq = jnp.zeros((1, QW), F32)
        for h in range(HL):
            taps[k : k + 1, h * DV : (h + 1) * DV] = tv[h : h + 1, :]
            pick_q = ((row + 2 * DK * h == col) & (row < 2 * DK)).astype(F32).astype(BF16)
            tq = tq + jnp.dot(tk, pick_q, preferred_element_type=F32)[h : h + 1, :]
        taps[k : k + 1, VW:] = tq

    wcopy.wait()
    gain = gain_ref[...].astype(F32)[None, :]
    for h in range(HL):
        for r in range(0, 160, 32):
            dst = VW + 32 * h if r == 0 else h * DV + r - 32
            src = h * 160 + r
            wg[dst : dst + 32, :] = (wv[src : src + 32, :].astype(F32) * gain).astype(BF16)

    def project(xt):
        xf = xt.astype(F32)
        scale = lax.rsqrt(jnp.mean(xf * xf, axis=-1, keepdims=True) + EPS)
        pr = lax.dot_general(xt, wg[...], (((1,), (1,)), ((), ())), preferred_element_type=F32)
        return (pr * scale).astype(BF16).astype(F32)

    for cp in tcopies:
        cp.wait()
    tl[8:, :] = project(xt8[...])

    pl.semaphore_wait(barrier, SEQ - 1 + TP - 1)
    halo = remote(tl.at[pl.ds(8 * NC, 8)], tl.at[pl.ds(0, 8)], halo_s, halo_r, (lax.rem(s + 1, SEQ), t))
    halo.start()
    wx = []
    for d in range(1, TP):
        cp = remote(
            wo_hbm.at[zc, yc, core], wf.at[TP - d, zc, yc, core], wx_s.at[d - 1], wx_r.at[d - 1], xpeer(d)
        )
        cp.start()
        wx.append(cp)

    def mix(i, c, dst):
        buf = pf.at[i % 2]
        buf[0:8, :] = tl[pl.ds(pl.multiple_of(c * 8, 8), 8), :]
        buf[8:, :] = project(xv[i])
        mixed = (
            buf[6 : 6 + C, :] * taps[0:1, :] + buf[7 : 7 + C, :] * taps[1:2, :] + buf[8 : 8 + C, :] * taps[2:3, :]
        )
        dst[...] = mixed.astype(BF16)

    def states(c, src):
        qe = jnp.concatenate(
            [jnp.transpose(src[:, VW:].astype(F32)).astype(BF16), jnp.ones((FP - QW, C), BF16)], axis=0
        )
        fk = (
            jnp.dot(ekv[0], qe, preferred_element_type=F32) * jnp.dot(ekv[1], qe, preferred_element_type=F32)
        ).astype(BF16)
        for h in range(HL):
            sc[c, h * F : (h + 1) * F, :] = jnp.dot(
                fk[h * F : (h + 1) * F, :], src[:, h * DV : (h + 1) * DV], preferred_element_type=F32
            )

    sent = []
    wa = []
    wb = {1: [], 2: [], 3: []}

    def onward(shard):
        n = 6 * (shard - 1)
        for d in range(1, 4):
            src = wf.at[shard, zc, :, core, :, 0:256]
            cp = remote(src, src, wb_s.at[n], wb_r.at[n], zpeer(d))
            cp.start()
            wb[shard].append(cp)
            src = wf.at[shard, :, yc, core, :, 256:512]
            cp = remote(src, src, wb_s.at[n + 1], wb_r.at[n + 1], ypeer(d))
            cp.start()
            wb[shard].append(cp)
            n += 2

    def across_cores(shard):
        for cp in wb[shard]:
            cp.wait()
        src = wf.at[shard, :, :, core]
        cp = remote(src, src, wc_s.at[shard - 1], wc_r.at[shard - 1], (sib, t))
        cp.start()
        return cp

    ekcopy.wait()
    for i, (d, half) in enumerate(tiles):
        c = near(d) * 2 + half
        if i == 3:
            halo.wait()
            tl[0:8, :] = jnp.where(s == 0, 0.0, tl[0:8, :])
        if i == 2:
            for cp in wx:
                cp.wait()
            for n in range(1, 4):
                src = wf.at[1:4, zc, yc, core, :, 0:256]
                cp = remote(src, src, wa_s.at[n - 1], wa_r.at[n - 1], ypeer(n))
                cp.start()
                wa.append(cp)
                src = wf.at[1:4, zc, yc, core, :, 256:512]
                cp = remote(src, src, wa_s.at[n + 2], wa_r.at[n + 2], zpeer(n))
                cp.start()
                wa.append(cp)
        if i == 5:
            for cp in wa:
                cp.wait()
            onward(1)
        xcopies[i].wait()
        tile = mx.at[i] if d else ga.at[t, half]
        mix(i, c, tile)
        if d:
            cp = remote(tile, ga.at[t, half], a_s.at[half, d - 1], a_r.at[half, d - 1], xpeer(d))
            cp.start()
            sent.append(cp)
        states(c, tile)

    run = jnp.zeros((HL * F, DV), F32)
    for c in range(NC):
        part = sc[c]
        if c % 2 == 0:
            sc[c] = run
        run = run + part
    for k in range(CHIPS):
        sb[k] = run[k * ROWS : (k + 1) * ROWS, :].astype(BF16)

    def spread(i, carry):
        k = lax.rem(chip + i, CHIPS)
        remote(sb.at[k], r1.at[s], s1_s, s1_r, (2 * k, t)).start()
        return carry

    lax.fori_loop(1, CHIPS, spread, 0)

    @pl.when(core == 1)
    def _():
        remote(sb.at[chip], r1.at[s], s3_s, s1_r, (s - 1, t)).start()

    @pl.when(core == 0)
    def _():
        r1[s] = sb[chip]

    eqcopy.wait()
    pos = lax.broadcasted_iota(jnp.int32, (C, C), 0) >= lax.broadcasted_iota(jnp.int32, (C, C), 1)

    def arrived(d, half):
        n = TP - d - 1
        remote(mx.at[0], ga.at[near(d), half], a_s.at[half, n], a_r.at[half, n], xpeer(d)).wait_recv()

    def scores(q, kt, h):
        parts = []
        if h > 0:
            parts.append(jnp.zeros((32 * h, C), BF16))
        parts.append(kt[32 * h + 16 : 32 * h + 32, :])
        parts.append(jnp.zeros((QW - 32 * h - 16, C), BF16))
        up = jnp.dot(q, jnp.concatenate(parts, axis=0), preferred_element_type=F32) + 1.0
        return up * up * 0.5 + 0.5

    def keys(src):
        return (jnp.transpose(src[:, VW:].astype(F32)) * 0.25).astype(BF16)

    def local(d, half):
        src = ga.at[near(d), half]
        q = src[:, VW:]
        qe = jnp.concatenate([q, jnp.ones((C, FP - QW), BF16)], axis=1)
        kt = keys(src)
        for h in range(HL):
            fq[half, d, :, h * FP : (h + 1) * FP] = (
                jnp.dot(qe, eqv[0, :, h * FP : (h + 1) * FP], preferred_element_type=F32)
                * jnp.dot(qe, eqv[1, :, h * FP : (h + 1) * FP], preferred_element_type=F32)
            ).astype(BF16)
            w = jnp.where(pos, scores(q, kt, h), 0.0).astype(BF16)
            nl[half, d, :, h * DV : (h + 1) * DV] = jnp.dot(
                w, src[:, h * DV : (h + 1) * DV], preferred_element_type=F32
            )

    def across(d):
        q = ga[near(d), 1, :, VW:]
        src = ga.at[near(d), 0]
        kt = keys(src)
        for h in range(HL):
            w = scores(q, kt, h).astype(BF16)
            nl[1, d, :, h * DV : (h + 1) * DV] += jnp.dot(
                w, src[:, h * DV : (h + 1) * DV], preferred_element_type=F32
            )

    local(0, 1)
    local(0, 0)
    across(0)

    @pl.when(core == 0)
    def _():
        pltpu.make_async_copy(r1.at[0 : SEQ - 1], r1.at[0 : SEQ - 1], s1_r).wait()
        acc = jnp.zeros((ROWS, DV), F32)
        for k in range(SEQ):
            p2[k // 2, k % 2] = acc.astype(BF16)
            acc = acc + r1[k].astype(F32)
        r2[chip] = p2[chip]

        def back(i, carry):
            k = lax.rem(chip + i, CHIPS)
            remote(p2.at[k], r2.at[chip], s2_s, s2_r, (2 * k, t)).start()
            return carry

        lax.fori_loop(1, CHIPS, back, 0)

    pltpu.make_async_copy(sb.at[0 : CHIPS - 1], sb.at[0 : CHIPS - 1], s1_s).wait()
    for d in (3, 1, 2):
        arrived(d, 1)
        local(d, 1)

    fwd = remote(r2, r2, s3_s, s3_r, (sib, t))

    @pl.when(core == 0)
    def _():
        pltpu.make_async_copy(p2.at[0 : CHIPS - 1], p2.at[0 : CHIPS - 1], s2_s).wait()
        pltpu.make_async_copy(r2.at[0 : CHIPS - 1], r2.at[0 : CHIPS - 1], s2_r).wait()
        fwd.start()

    @pl.when(core == 1)
    def _():
        remote(sb.at[chip], r1.at[s], s3_s, s1_r, (s - 1, t)).wait_send()
        fwd.wait_recv()

    pcopies = []
    for d in (1, 3, 2, 0):
        n = near(d)
        for k in range(CHIPS):
            h, o = k // 4, (k % 4) * ROWS
            val = (r2[k, core].astype(F32) + sc[2 * n, k * ROWS : (k + 1) * ROWS, :]).astype(BF16)
            if d:
                ps[d - 1, h, o : o + ROWS, :] = val
            else:
                pp[t, h, o : o + ROWS, :] = val
        if d:
            cp = remote(ps.at[d - 1], pp.at[t, :, 0:F, :], q_s.at[d - 1], q_r.at[d - 1], xpeer(d))
            cp.start()
            pcopies.append(cp)
    wc = {1: across_cores(1)}
    onward(3)
    onward(2)

    for d in (3, 1, 2):
        arrived(d, 0)
        local(d, 0)
        across(d)

    @pl.when(core == 0)
    def _():
        fwd.wait_send()

    for cp in pcopies:
        cp.wait()

    wc[3] = across_cores(3)
    results = []
    own = []
    for half in range(2):
        for d in range(TP):
            for h in range(HL):
                num = nl[half, d, :, h * DV : (h + 1) * DV] + jnp.dot(
                    fq[half, d, :, h * FP : (h + 1) * FP], pp[near(d), h], preferred_element_type=F32
                )
                spread_ = jnp.mean(num * num, axis=-1, keepdims=True)
                gh[half, d, :, h * DV : (h + 1) * DV] = (num * lax.rsqrt(spread_ + EPS)).astype(BF16)
        for n, d in enumerate((1, 3, 2, 0)):
            if half == 0:
                if n == 1:
                    wc[2] = across_cores(2)
                if d:
                    wc[d].wait()
                else:
                    wocopy.wait()
            acc = jnp.zeros((C, 512), F32)
            for p in range(TP):
                acc = acc + jnp.dot(
                    gh[half, p], wf[d, near(p)].reshape(512, 512), preferred_element_type=F32
                )
            ob[half, n] = acc.astype(BF16)
            rows = out_ref.at[pl.ds(pl.multiple_of(t * 512 + half * C, C), C)]
            if d:
                cp = remote(ob.at[half, n], rows, b_s.at[half, d - 1], b_r.at[half, d - 1], xpeer(d))
                cp.start()
                results.append(cp)
            else:
                cp = pltpu.make_async_copy(ob.at[half, n], rows, own_s.at[half])
                cp.start()
                own.append(cp)

    for cp in sent + results:
        cp.wait_send()
    for half in range(2):
        for d in range(1, TP):
            rows = out_ref.at[pl.ds(pl.multiple_of(near(TP - d) * 512 + half * C, C), C)]
            remote(ob.at[half, 0], rows, b_s.at[half, 0], b_r.at[half, d - 1], xpeer(d)).wait_recv()
    for cp in own:
        cp.wait()


def copy_kernel(src_ref, dst_ref, buf, in_sem, out_sem):
    loads, stores = [], []
    for i in range(8):
        rows = pl.ds(i * (T // 8), T // 8)
        loads.append(pltpu.make_async_copy(src_ref.at[rows], buf.at[rows], in_sem.at[i]))
        stores.append(pltpu.make_async_copy(buf.at[rows], dst_ref.at[rows], out_sem.at[i]))
    for cp in loads:
        cp.start()
    for load, store in zip(loads, stores):
        load.wait()
        store.start()
    for cp in stores:
        cp.wait()


def body(tokens, gain, w_in, conv_taps, w_out):
    wt = jnp.transpose(w_in, (1, 2, 0)).reshape(HL * 160, D)
    eq, ek = feature_maps()
    hbm = pl.BlockSpec(memory_space=pl.ANY)
    vmem = pl.BlockSpec(memory_space=pltpu.VMEM)
    dma = pltpu.SemaphoreType.DMA
    width = VW + QW
    result = pl.pallas_call(
        kernel,
        out_shape=jax.ShapeDtypeStruct((T, 512), BF16),
        in_specs=[hbm, vmem, hbm, vmem, hbm, hbm, hbm],
        out_specs=hbm,
        scratch_shapes=[
            pltpu.VMEM((NC, C, D), BF16),
            pltpu.VMEM((8 * NC, D), BF16),
            pltpu.VMEM((width, D), BF16),
            pltpu.VMEM((width, D), BF16),
            pltpu.VMEM((2, FP, HL * FP), BF16),
            pltpu.VMEM((2, HL * F, FP), BF16),
            pltpu.VMEM((8, width), F32),
            pltpu.VMEM((2, 8 + C, width), F32),
            pltpu.VMEM((8 + 8 * NC, width), F32),
            pltpu.VMEM((6, C, width), BF16),
            pltpu.VMEM((TP, 2, C, width), BF16),
            pltpu.VMEM((NC, HL * F, DV), F32),
            pltpu.VMEM((2, TP, C, VW), F32),
            pltpu.VMEM((2, TP, C, HL * FP), BF16),
            pltpu.VMEM((CHIPS, ROWS, DV), BF16),
            pltpu.VMEM((SEQ, ROWS, DV), BF16),
            pltpu.VMEM((CHIPS, 2, ROWS, DV), BF16),
            pltpu.VMEM((CHIPS, 2, ROWS, DV), BF16),
            pltpu.VMEM((3, HL, F, DV), BF16),
            pltpu.VMEM((TP, HL, FP, DV), BF16),
            pltpu.VMEM((4, 4, 4, 2, 64, 512), BF16),
            pltpu.VMEM((2, TP, C, VW), BF16),
            pltpu.VMEM((2, 4, C, 512), BF16),
            dma((3 + NC,)), dma((NC,)), dma, dma, dma, dma, dma, dma, dma, dma, dma,
            dma((3,)), dma((3,)), dma((6,)), dma((6,)), dma((18,)), dma((18,)), dma((3,)), dma((3,)),
            dma((2, 3)), dma((2, 3)), dma((3,)), dma((3,)), dma((2, 3)), dma((2, 3)), dma((2,)),
        ],
        compiler_params=pltpu.CompilerParams(
            collective_id=0, has_side_effects=True, vmem_limit_bytes=59 * 1024 * 1024
        ),
    )(
        tokens, gain, wt, conv_taps, w_out.reshape(4, 4, 2, 64, 512),
        jnp.asarray(eq), jnp.asarray(ek),
    )
    return pl.pallas_call(
        copy_kernel,
        out_shape=jax.ShapeDtypeStruct((T, 512), BF16),
        in_specs=[hbm],
        out_specs=hbm,
        scratch_shapes=[pltpu.VMEM((T, 512), BF16), dma((8,)), dma((8,))],
    )(result)


def solution(mesh):
    return jax.shard_map(
        body,
        mesh=mesh,
        in_specs=(P("seq", None), P(), P(None, "tp", None), P(None, "tp", None), P(None, "tp")),
        out_specs=P("seq", "tp"),
        check_vma=False,
    )
```
